32 devices in a mesh: tok: 8 (over z, core), rep: 4 (over y, x).
Axes of the slice: x: 2, y: 2, z: 4, core: 2. Of those that a mesh axis runs over, the one named last changes fastest.
Arguments:
- hidden_in: bfloat16 [4096, 4096], P('tok', 'rep'), may hold values from -9 to 9
- w_query: bfloat16 [4096, 4096], P(None, 'rep'), may hold values from -2 to 2
- w_key: bfloat16 [4096, 4096], P(None, 'rep'), may hold values from -2 to 2
- w_value: bfloat16 [4096, 4096], P(None, 'rep'), may hold values from -0.09375 to 0.09375
- w_out: bfloat16 [4096, 4096], P('rep'), may hold values from -3 to 3
- q_gain: float32 [4096], P('rep'), may hold values from 0.5 to 6
- k_gain: float32 [4096], P('rep'), may hold values from 0.5 to 6
- post_gain: float32 [4096], P('rep'), may hold values from 0.1 to 1.9
- prompt_lengths: int32 [8], replicated, may hold values from 1 to 2048, as said below
- segment_ids: int32 [4096], replicated, may hold values from 0 to 7, as said below
- deal: int32 [4096], replicated, may hold values from 0 to 4095, as said below
- inverse: int32 [4096], replicated, may hold values from 0 to 4095, as said below
- slots: int32 [4096], replicated, may hold values from 0 to 4095, as said below
Outputs:
- output: bfloat16 [4096, 4096], P('tok', 'rep')
- cache_keys: bfloat16 [4096, 4096], P('tok', 'rep')
- cache_values: bfloat16 [4096, 4096], P('tok', 'rep')
The draws below stay inside these ranges and needn't reach their ends.
Inputs may be any that keep to these rules, and one draw needn't show every extreme that they name: `prompt_lengths`: the lengths sum to 4096; the longest prompt has exactly 2048 tokens. `segment_ids`: prompts lie in order: prompt s holds the prompt_lengths[s] packed tokens after those of prompts 0 to s - 1. `deal`: A permutation. For any two indices a and b of tok, exactly 64 of the packed tokens a * 512 to (a + 1) * 512 - 1 sit in dealt rows b * 512 to (b + 1) * 512 - 1. inverse[deal[q]] = q for every dealt row q. `slots`: A permutation. For any two indices a and b of tok, exactly 64 of the dealt rows a * 512 to (a + 1) * 512 - 1 have cache rows b * 512 to (b + 1) * 512 - 1.
All inputs are finite; a program needn't handle non-finite values.
Results may differ from the reference program's by a relative error of at most 0.012.
Values may be sent and summed in bfloat16 or wider, within the bound.
A program may use at most 128 MiB of HBM per device.

```python
import math
import jax
import jax.numpy as jnp
from jax import lax

D = 4096
HEADS = 32
HEAD_DIM = 128
TOK_DEV = 512
NSEG = 8
TOKENS = 4096
MAXLEN = 2048


def bounded(key, shape):
    return jax.random.truncated_normal(key, -3.0, 3.0, shape, jnp.float32)


def projection_pair(key):
    lower_draw = bounded(jax.random.fold_in(key, 11), (D, D))
    upper_draw = bounded(jax.random.fold_in(key, 12), (D, D))
    wobble = jnp.exp(jax.random.uniform(jax.random.fold_in(key, 13), (1, D), jnp.float32, -0.7, 0.7))
    head_index = jnp.arange(HEADS, dtype=jnp.float32)
    head_scale = 0.6 * 3.0 ** (head_index / max(HEADS - 1, 1))
    scale = jnp.repeat(head_scale, HEAD_DIM)[None, :] * wobble / math.sqrt(D)
    key_part = upper_draw
    return (lower_draw * scale, key_part * scale)


def draw_w_query(key, part):
    return projection_pair(key)[0].astype(jnp.bfloat16)


def draw_w_key(key, part):
    return projection_pair(key)[1].astype(jnp.bfloat16)


def draw_w_out(key, part):
    base = bounded(jax.random.fold_in(key, 41), (D, D))
    columns = jnp.arange(D, dtype=jnp.float32)[None, :]
    scale = 0.6 * 3.0 ** (columns / max(D - 1, 1)) * jnp.exp(jax.random.uniform(jax.random.fold_in(key, 43), (1, D), jnp.float32, -0.7, 0.7))
    values = base * scale
    return (values / math.sqrt(D)).astype(jnp.bfloat16)


def draw_hidden_in(key, part):
    noise = bounded(jax.random.fold_in(key, 51), (TOKENS, D))
    row_scale = jnp.exp(jax.random.uniform(jax.random.fold_in(key, 53), (TOKENS, 1), jnp.float32, -0.7, 0.7))
    values = noise * row_scale
    return values.astype(jnp.bfloat16)


def gain_draw(key, salt):
    low_end, high_end = (0.5, 2.0)
    logs = jax.random.uniform(jax.random.fold_in(key, salt), (D,), jnp.float32, math.log(low_end), math.log(high_end))
    return jnp.exp(logs)


def draw_q_gain(key, part):
    return gain_draw(key, 61)


def draw_k_gain(key, part):
    return gain_draw(key, 62)


def pack_layout(key):
    remainder = TOKENS - MAXLEN
    picks = jax.random.permutation(jax.random.fold_in(key, 21), remainder - 1)[:NSEG - 2] + 1
    cuts = jnp.sort(picks.astype(jnp.int32))
    edges = jnp.concatenate([jnp.zeros((1,), jnp.int32), cuts, jnp.full((1,), remainder, jnp.int32)])
    pieces = edges[1:] - edges[:-1]
    lengths = jnp.concatenate([jnp.full((1,), MAXLEN, jnp.int32), pieces])
    offset = jax.random.randint(jax.random.fold_in(key, 22), (), 0, NSEG)
    lengths = jnp.roll(lengths, offset)
    prompt_ends = jnp.cumsum(lengths)
    token_ids = jnp.arange(TOKENS, dtype=jnp.int32)
    segments = jnp.sum((token_ids[:, None] >= prompt_ends[None, :]).astype(jnp.int32), axis=1)
    return (lengths, segments)


def draw_prompt_lengths(key, part):
    return pack_layout(key)[0]


def draw_segment_ids(key, part):
    return pack_layout(key)[1]


def deal_layout(key):
    shards = TOKENS // TOK_DEV
    group_size = TOK_DEV // shards

    def ranking(salt):
        split_keys = jax.random.split(jax.random.fold_in(key, salt), shards)
        return jax.vmap(lambda single: jax.random.permutation(single, TOK_DEV))(split_keys).astype(jnp.int32)

    def spread(ranks, within_order):
        target = ranks // group_size
        within = ranks % group_size
        source = jnp.arange(shards, dtype=jnp.int32)[:, None]
        placed = within_order[target, source * group_size + within]
        return (target * TOK_DEV + placed).reshape(-1).astype(jnp.int32)
    inverse_rows = spread(ranking(31), ranking(32))
    deal_rows = jnp.argsort(inverse_rows).astype(jnp.int32)
    slot_rows = spread(ranking(33), ranking(34))
    return (deal_rows, inverse_rows, slot_rows)


def draw_deal(key, part):
    return deal_layout(key)[0]


def draw_inverse(key, part):
    return deal_layout(key)[1]


def draw_slots(key, part):
    return deal_layout(key)[2]


def shard_levels(key, dims, cuts, low, largest):
    level, own = 1.0, jax.random.fold_in(key, 6)
    for axis_at, parts in cuts:
        draws = jnp.exp(jax.random.uniform(jax.random.fold_in(own, axis_at), (parts,), jnp.float32, low / len(cuts), largest / len(cuts)))
        level = level * jnp.repeat(draws, dims[axis_at] // parts).reshape([-1 if axis == axis_at else 1 for axis in range(len(dims))])
    return level


def gaussian(rng, extent, deviation, most, cuts=(), kind=jnp.bfloat16):
    values = jax.random.normal(rng, extent, jnp.float32) * deviation
    if len(cuts) > 0:
        values = shard_levels(rng, extent, cuts, -0.22, 0.18) * values
    return jnp.clip(values, min=-most, max=most).astype(kind)


def setup_inputs(seed: int = 0) -> dict:
    key_list = jax.random.split(jax.random.key(seed), 14)
    return {
        "hidden_in": draw_hidden_in(jax.random.fold_in(key_list[13], 71), 0),
        "w_query": draw_w_query(jax.random.fold_in(key_list[13], 71), 0),
        "w_key": draw_w_key(jax.random.fold_in(key_list[13], 71), 0),
        "w_value": gaussian(key_list[3], (D, D), D ** -0.5, 0.09375, ((1, 4),)),
        "w_out": draw_w_out(jax.random.fold_in(key_list[13], 71), 0),
        "q_gain": draw_q_gain(jax.random.fold_in(key_list[13], 71), 0),
        "k_gain": draw_k_gain(jax.random.fold_in(key_list[13], 71), 0),
        "post_gain": jnp.clip(1.0 + 0.18 * jax.random.normal(key_list[7], (D,), jnp.float32), 0.1, 1.9),
        "prompt_lengths": draw_prompt_lengths(jax.random.fold_in(key_list[13], 71), 0),
        "segment_ids": draw_segment_ids(jax.random.fold_in(key_list[13], 71), 0),
        "deal": draw_deal(jax.random.fold_in(key_list[13], 71), 0),
        "inverse": draw_inverse(jax.random.fold_in(key_list[13], 71), 0),
        "slots": draw_slots(jax.random.fold_in(key_list[13], 71), 0),
    }


EPSILON = 1e-06
ROPE_BASE = 500000.0

def rotate(values, positions):
    half_size = values.shape[-1] // 2
    frequency = ROPE_BASE ** (-jnp.arange(half_size, dtype=jnp.float32) * 2.0 / values.shape[-1])
    angles = positions.astype(jnp.float32)[:, None] * frequency[None, :]
    cosine = jnp.cos(angles)[:, None, :]
    sine_part = jnp.sin(angles)[:, None, :]
    lower_half = values[..., :half_size]
    upper_half = values[..., half_size:]
    return jnp.concatenate([lower_half * cosine - upper_half * sine_part, upper_half * cosine + lower_half * sine_part], axis=-1)

def reference(hidden_in, w_query, w_key, w_value, w_out, q_gain, k_gain, post_gain, prompt_lengths, segment_ids, deal, inverse, slots):
    packed = hidden_in[inverse]
    query_rows = jnp.dot(packed, w_query, preferred_element_type=jnp.float32)
    key_rows = jnp.dot(packed, w_key, preferred_element_type=jnp.float32)
    value_half = jnp.dot(packed, w_value, preferred_element_type=jnp.float32).astype(jnp.bfloat16)
    prompt_starts = jnp.cumsum(prompt_lengths) - prompt_lengths
    token_ids = jnp.arange(TOKENS, dtype=jnp.int32)
    positions = token_ids - prompt_starts[segment_ids]
    query_rows = query_rows * lax.rsqrt(lax.optimization_barrier(jnp.mean(query_rows * query_rows, axis=1, keepdims=True)) + EPSILON) * q_gain[None, :]
    key_rows = key_rows * lax.rsqrt(lax.optimization_barrier(jnp.mean(key_rows * key_rows, axis=1, keepdims=True)) + EPSILON) * k_gain[None, :]
    query_rot = rotate(query_rows.reshape(TOKENS, HEADS, HEAD_DIM), positions).astype(jnp.bfloat16)
    key_rot = rotate(key_rows.reshape(TOKENS, HEADS, HEAD_DIM), positions).astype(jnp.bfloat16)
    allowed = (segment_ids[:, None] == segment_ids[None, :]) & (token_ids[None, :] <= token_ids[:, None])
    scale = HEAD_DIM ** (-0.5)

    def one_head(operands):
        head_query, head_key, head_value = operands
        scores = jnp.dot(head_query.astype(jnp.float32), head_key.astype(jnp.float32).T) * scale
        masked = jnp.where(allowed, scores, -1e+30)
        row_top = lax.optimization_barrier(jnp.max(masked, axis=1, keepdims=True))
        weights = jnp.where(allowed, jnp.exp(masked - row_top), 0.0)
        totals = lax.optimization_barrier(jnp.sum(weights, axis=1, keepdims=True))
        rounded = lax.optimization_barrier(weights.astype(jnp.bfloat16))
        return jnp.dot(rounded.astype(jnp.float32), head_value.astype(jnp.float32)) / totals
    value_heads = value_half.reshape(TOKENS, HEADS, HEAD_DIM)
    per_head = lax.map(one_head, (query_rot.transpose(1, 0, 2), key_rot.transpose(1, 0, 2), value_heads.transpose(1, 0, 2)))
    attended = per_head.transpose(1, 0, 2).reshape(TOKENS, D).astype(jnp.bfloat16)
    mixed = jnp.dot(attended, w_out, preferred_element_type=jnp.float32)
    normed = mixed * lax.rsqrt(lax.optimization_barrier(jnp.mean(mixed * mixed, axis=1, keepdims=True)) + EPSILON) * post_gain[None, :]
    output = (packed.astype(jnp.float32) + normed).astype(jnp.bfloat16)
    key_flat = key_rot.reshape(TOKENS, D)
    cache_keys = jnp.zeros((TOKENS, D), jnp.bfloat16).at[slots].set(key_flat[deal])
    cache_values = jnp.zeros((TOKENS, D), jnp.bfloat16).at[slots].set(value_half[deal])
    return (output, cache_keys, cache_values)
```

```python
import functools
import math

import jax
import jax.numpy as jnp
from jax import lax
from jax.experimental import pallas as pl
from jax.experimental.pallas import tpu as pltpu
from jax.sharding import PartitionSpec as P

HEAD_DIM = 128


EPSILON = 1e-06
ROPE_BASE = 500000.0


def rotate(values, positions):
    half_size = values.shape[-1] // 2
    frequency = ROPE_BASE ** (-jnp.arange(half_size, dtype=jnp.float32) * 2.0 / values.shape[-1])
    angles = positions.astype(jnp.float32)[:, None] * frequency[None, :]
    cosine = jnp.cos(angles)[:, None, :]
    sine_part = jnp.sin(angles)[:, None, :]
    lower_half = values[..., :half_size]
    upper_half = values[..., half_size:]
    return jnp.concatenate(
        [
            lower_half * cosine - upper_half * sine_part,
            upper_half * cosine + lower_half * sine_part,
        ],
        axis=-1,
    )


def bucketed(table_rows, row_order, shards):
    picked = table_rows[row_order]
    return picked.reshape(shards, picked.shape[0] // shards, picked.shape[1])


def placement_order(sources, shard_rows):
    local_ids = jnp.arange(sources.shape[0], dtype=jnp.int32)
    arrival = jnp.argsort(sources * shard_rows + local_ids)
    return jnp.argsort(arrival)


def body(
    hidden_in,
    w_query,
    w_key,
    w_value,
    w_out,
    q_gain,
    k_gain,
    post_gain,
    prompt_lengths,
    segment_ids,
    deal,
    inverse,
    slots,
):
    tok_rows, width_dev = hidden_in.shape
    full_width = w_query.shape[0]
    head_size = HEAD_DIM
    heads_dev = width_dev // head_size
    shards = lax.axis_size("tok")
    first_row = lax.axis_index("tok") * tok_rows
    my_packed = lax.dynamic_slice_in_dim(deal, first_row, tok_rows)
    my_segment = segment_ids[my_packed]
    prompt_ids = jnp.arange(prompt_lengths.shape[0], dtype=jnp.int32)
    prompt_starts = jnp.cumsum(prompt_lengths) - prompt_lengths
    my_start = jnp.sum(
        jnp.where(my_segment[:, None] == prompt_ids[None, :], prompt_starts[None, :], 0), axis=1
    )
    positions = my_packed - my_start
    pieces = lax.all_gather(hidden_in, "rep", axis=1, tiled=True)
    query_rows = jnp.dot(pieces, w_query, preferred_element_type=jnp.float32)
    key_rows = jnp.dot(pieces, w_key, preferred_element_type=jnp.float32)
    value_rows = jnp.dot(pieces, w_value, preferred_element_type=jnp.float32)
    query_sums, key_sums = lax.psum(
        (jnp.sum(query_rows * query_rows, axis=1), jnp.sum(key_rows * key_rows, axis=1)), "rep"
    )
    query_rows = (
        query_rows * lax.rsqrt(query_sums / full_width + EPSILON)[:, None] * q_gain[None, :]
    )
    key_rows = key_rows * lax.rsqrt(key_sums / full_width + EPSILON)[:, None] * k_gain[None, :]
    query_rot = rotate(query_rows.reshape(tok_rows, heads_dev, head_size), positions).astype(
        jnp.bfloat16
    )
    key_rot = (
        rotate(key_rows.reshape(tok_rows, heads_dev, head_size), positions)
        .astype(jnp.bfloat16)
        .reshape(tok_rows, width_dev)
    )
    value_half = value_rows.astype(jnp.bfloat16)
    scale = head_size ** (-0.5)

    def attend(state_now, key_block, value_block, key_packed):
        row_top, totals, weighted = state_now
        block_keys = key_block.reshape(key_block.shape[0], heads_dev, head_size)
        block_values = value_block.reshape(value_block.shape[0], heads_dev, head_size)
        key_segment = segment_ids[key_packed]
        allowed = (key_segment[None, :] == my_segment[:, None]) & (
            key_packed[None, :] <= my_packed[:, None]
        )
        scores = (
            jnp.einsum("qhd,khd->hqk", query_rot, block_keys, preferred_element_type=jnp.float32)
            * scale
        )
        masked = jnp.where(allowed[None], scores, -1e30)
        new_top = jnp.maximum(row_top, jnp.max(masked, axis=2))
        weights = jnp.where(allowed[None], jnp.exp(masked - new_top[:, :, None]), 0.0)
        factor = jnp.exp(row_top - new_top)
        totals = totals * factor + jnp.sum(weights, axis=2)
        weighted = weighted * factor[:, :, None] + jnp.einsum(
            "hqk,khd->hqd",
            weights.astype(jnp.bfloat16),
            block_values,
            preferred_element_type=jnp.float32,
        )
        return (new_top, totals, weighted)

    start_state = (
        jnp.full((heads_dev, tok_rows), -1e30, jnp.float32),
        jnp.zeros((heads_dev, tok_rows), jnp.float32),
        jnp.zeros((heads_dev, tok_rows, head_size), jnp.float32),
    )
    owned_rows = lax.dynamic_slice_in_dim(jnp.argsort(slots), first_row, tok_rows)
    my_slots = lax.dynamic_slice_in_dim(slots, first_row, tok_rows)
    slot_order = jnp.argsort(my_slots)
    sent_keys, sent_values = (
        lax.all_to_all(
            bucketed(key_rot, slot_order, shards), "tok", split_axis=0, concat_axis=0, tiled=True
        ),
        lax.all_to_all(
            bucketed(value_half, slot_order, shards), "tok", split_axis=0, concat_axis=0, tiled=True
        ),
    )
    arrival = placement_order(owned_rows // tok_rows, tok_rows)
    cache_keys = sent_keys.reshape(tok_rows, width_dev)[arrival]
    cache_values = sent_values.reshape(tok_rows, width_dev)[arrival]
    pieces = (
        lax.all_gather(key_rot, "tok", axis=0, tiled=True),
        lax.all_gather(value_half, "tok", axis=0, tiled=True),
    )
    key_all = pieces[0]
    block_size = math.gcd(key_all.shape[0], tok_rows)
    block_count = key_all.shape[0] // block_size

    def advance(state_in, block_set):
        return (attend(state_in, block_set[0], block_set[1], block_set[2]), None)

    state_out, _ = lax.scan(
        advance,
        start_state,
        (
            key_all.reshape(block_count, block_size, width_dev),
            pieces[1].reshape(block_count, block_size, width_dev),
            deal.reshape(block_count, block_size),
        ),
    )
    row_top, totals, weighted = state_out
    attended = (
        (weighted / totals[:, :, None])
        .transpose(1, 0, 2)
        .reshape(tok_rows, width_dev)
        .astype(jnp.bfloat16)
    )
    mixed_rows = (
        lax.psum_scatter(
            lax.dot_general(
                w_out, attended, (((0,), (1,)), ((), ())), preferred_element_type=jnp.float32
            ).astype(jnp.bfloat16),
            "rep",
            scatter_dimension=0,
            tiled=True,
        )
        .astype(jnp.float32)
        .T
    )
    mixed_sums = lax.psum(jnp.sum(mixed_rows * mixed_rows, axis=1), "rep")
    normed_rows = (
        mixed_rows * lax.rsqrt(mixed_sums / full_width + EPSILON)[:, None] * post_gain[None, :]
    )
    result_rows = (hidden_in.astype(jnp.float32) + normed_rows).astype(jnp.bfloat16)
    packed_order = jnp.argsort(my_packed)
    returned = lax.all_to_all(
        bucketed(result_rows, packed_order, shards), "tok", split_axis=0, concat_axis=0, tiled=True
    )
    my_dealt = lax.dynamic_slice_in_dim(inverse, first_row, tok_rows)
    output = returned.reshape(tok_rows, width_dev)[placement_order(my_dealt // tok_rows, tok_rows)]
    return (output, cache_keys, cache_values)


def select_rows(hits, rows):
    return jnp.dot(
        hits.astype(jnp.bfloat16), rows, preferred_element_type=jnp.float32
    ).astype(jnp.bfloat16)


def attend_kernel(starts_ref, target_ref, qk_ref, v_ref, out_ref, keys, values, *, size, head_size):
    block = pl.program_id(0)
    mine = pl.ds(pl.multiple_of(block * size, size), size)
    row_iota = lax.broadcasted_iota(jnp.int32, (size, size), 0)
    column_iota = lax.broadcasted_iota(jnp.int32, (size, size), 1)
    hits = jnp.where(row_iota == target_ref[0], 1.0, 0.0).astype(jnp.bfloat16)
    qk_rows = qk_ref[...].reshape(size, 2 * head_size)
    v_rows = v_ref[...].reshape(size, head_size)
    packed_qk = jnp.dot(hits, qk_rows, preferred_element_type=jnp.float32).astype(jnp.bfloat16)
    packed_v = jnp.dot(hits, v_rows, preferred_element_type=jnp.float32).astype(jnp.bfloat16)
    query = packed_qk[:, :head_size]
    keys[mine, :] = packed_qk[:, head_size:]
    values[mine, :] = packed_v
    first = block * size
    rows = first + lax.broadcasted_iota(jnp.int32, (size, 1), 0)
    row_start = jnp.zeros((size, 1), jnp.int32)
    low = jnp.int32(0)
    for prompt in range(starts_ref.shape[0]):
        start = starts_ref[prompt]
        row_start = jnp.where(rows >= start, jnp.maximum(row_start, start), row_start)
        low = jnp.where(first >= start, jnp.maximum(low, start), low)
    scale = head_size ** (-0.5) * math.log2(math.e)

    def scores_of(key_rows):
        return lax.dot_general(
            query, key_rows, (((1,), (1,)), ((), ())), preferred_element_type=jnp.float32
        ) * scale

    local_start = row_start - first
    allowed = (column_iota >= local_start) & (column_iota <= row_iota)
    scores = jnp.where(allowed, scores_of(packed_qk[:, head_size:]), -1e30)
    top = jnp.max(scores, axis=1, keepdims=True)
    weights = jnp.exp2(scores - top)
    totals = jnp.sum(weights, axis=1, keepdims=True)
    weighted = jnp.dot(
        weights.astype(jnp.bfloat16), packed_v, preferred_element_type=jnp.float32
    )

    def earlier(step, state):
        top, totals, weighted = state
        base = pl.multiple_of((block - 1 - step) * size, size)
        scores = scores_of(keys[pl.ds(base, size), :])
        scores = jnp.where(column_iota >= row_start - base, scores, -1e30)
        new_top = jnp.maximum(top, jnp.max(scores, axis=1, keepdims=True))
        factor = jnp.exp2(top - new_top)
        weights = jnp.exp2(scores - new_top)
        totals = totals * factor + jnp.sum(weights, axis=1, keepdims=True)
        weighted = weighted * factor + jnp.dot(
            weights.astype(jnp.bfloat16),
            values[pl.ds(base, size), :],
            preferred_element_type=jnp.float32,
        )
        return (new_top, totals, weighted)

    top, totals, weighted = lax.fori_loop(
        0, block - low // size, earlier, (top, totals, weighted)
    )
    out_ref[...] = (weighted / totals).astype(jnp.bfloat16)


def attend_head(starts, target, qk_rows, v_rows):
    shards, tok_rows, head_size = v_rows.shape
    chunk = tok_rows // shards
    return pl.pallas_call(
        functools.partial(attend_kernel, size=tok_rows, head_size=head_size),
        out_shape=jax.ShapeDtypeStruct((shards * tok_rows, head_size), jnp.bfloat16),
        grid_spec=pltpu.PrefetchScalarGridSpec(
            num_scalar_prefetch=1,
            grid=(shards,),
            in_specs=[
                pl.BlockSpec((1, 1, tok_rows), lambda i, s: (i, 0, 0)),
                pl.BlockSpec((shards, chunk, 2 * head_size), lambda i, s: (0, i, 0)),
                pl.BlockSpec((shards, chunk, head_size), lambda i, s: (0, i, 0)),
            ],
            out_specs=pl.BlockSpec((tok_rows, head_size), lambda i, s: (i, 0)),
            scratch_shapes=[
                pltpu.VMEM((shards * tok_rows, head_size), jnp.bfloat16),
                pltpu.VMEM((shards * tok_rows, head_size), jnp.bfloat16),
            ],
        ),
        compiler_params=pltpu.CompilerParams(
            dimension_semantics=("arbitrary",), vmem_limit_bytes=48 << 20
        ),
        cost_estimate=pl.CostEstimate(
            flops=8 * tok_rows * tok_rows * shards * head_size * 3,
            bytes_accessed=8 * shards * tok_rows * head_size,
            transcendentals=3 * shards * tok_rows * tok_rows,
        ),
    )(starts, target, qk_rows, v_rows)


def body_heads(
    hidden_in,
    w_query,
    w_key,
    w_value,
    w_out,
    q_gain,
    k_gain,
    post_gain,
    prompt_lengths,
    segment_ids,
    deal,
    inverse,
    slots,
):
    tok_rows, width_dev = hidden_in.shape
    full_width = w_query.shape[0]
    head_size = HEAD_DIM
    heads_dev = width_dev // head_size
    shards = lax.axis_size("tok")
    chunk = tok_rows // shards
    me = lax.axis_index("tok")
    first_row = me * tok_rows
    pieces = lax.all_gather(hidden_in, "rep", axis=1, tiled=True)

    local = jnp.arange(tok_rows, dtype=jnp.int32)
    starts = jnp.cumsum(prompt_lengths) - prompt_lengths
    my_packed = lax.dynamic_slice_in_dim(deal, first_row, tok_rows)
    my_slots = lax.dynamic_slice_in_dim(slots, first_row, tok_rows)
    rank = jnp.sum((my_packed[None, :] < my_packed[:, None]).astype(jnp.int32), axis=1)
    sort_hits = rank[None, :] == local[:, None]
    sorted_packed = jnp.sum(jnp.where(sort_hits, my_packed[None, :], 0), axis=1)
    sorted_slots = jnp.sum(jnp.where(sort_hits, my_slots[None, :], 0), axis=1)
    my_start = jnp.max(
        jnp.where(starts[None, :] <= sorted_packed[:, None], starts[None, :], 0), axis=1
    )
    positions = sorted_packed - my_start

    source = inverse.reshape(shards, tok_rows) // tok_rows
    before = (source[:, None, :] == source[:, :, None]) & (local[None, None, :] < local[None, :, None])
    arrived = source * chunk + jnp.sum(before.astype(jnp.int32), axis=2)
    target = jnp.sum(
        jnp.where(arrived[:, :, None] == local[None, None, :], local[None, :, None], 0), axis=1
    )

    slot_rank = jnp.sum((sorted_slots[None, :] < sorted_slots[:, None]).astype(jnp.int32), axis=1)
    slot_hits = slot_rank[None, :] == local[:, None]
    slot_rows = slots.reshape(shards, tok_rows) - first_row
    owned = (slot_rows >= 0) & (slot_rows < tok_rows)
    ahead = owned[:, None, :] & (slot_rows[:, None, :] < slot_rows[:, :, None])
    landed = jnp.arange(shards, dtype=jnp.int32)[:, None] * chunk + jnp.sum(
        ahead.astype(jnp.int32), axis=2
    )
    landed = jnp.where(owned, landed, -1).reshape(-1)
    slot_target = jnp.sum(
        jnp.where(landed[:, None] == local[None, :], slot_rows.reshape(-1)[:, None], 0), axis=0
    )

    sent_hidden = lax.all_to_all(
        select_rows(sort_hits, hidden_in).reshape(shards, chunk, width_dev),
        "tok",
        split_axis=0,
        concat_axis=0,
        tiled=True,
    )
    my_target = lax.dynamic_index_in_dim(target, me, 0, keepdims=False)
    my_hits = my_target[None, :] == local[:, None]
    packed_hidden = select_rows(my_hits, sent_hidden.reshape(tok_rows, width_dev))

    pieces = select_rows(sort_hits, pieces)
    query_rows = jnp.dot(pieces, w_query, preferred_element_type=jnp.float32)
    key_rows = jnp.dot(pieces, w_key, preferred_element_type=jnp.float32)
    sums = jnp.stack(
        [jnp.sum(query_rows * query_rows, axis=1), jnp.sum(key_rows * key_rows, axis=1)]
    )
    sums = lax.psum(sums, "rep")
    value_half = jnp.dot(pieces, w_value, preferred_element_type=jnp.float32).astype(jnp.bfloat16)
    query_rows = query_rows * lax.rsqrt(sums[0] / full_width + EPSILON)[:, None] * q_gain[None, :]
    key_rows = key_rows * lax.rsqrt(sums[1] / full_width + EPSILON)[:, None] * k_gain[None, :]
    query_rot = rotate(query_rows.reshape(tok_rows, heads_dev, head_size), positions).astype(
        jnp.bfloat16
    )
    key_rot = rotate(key_rows.reshape(tok_rows, heads_dev, head_size), positions).astype(
        jnp.bfloat16
    )
    v_rows = lax.all_to_all(
        value_half.reshape(tok_rows, heads_dev, head_size).transpose(1, 0, 2),
        "tok",
        split_axis=0,
        concat_axis=0,
        tiled=True,
    )
    qk_rows = lax.all_to_all(
        jnp.concatenate([query_rot, key_rot], axis=2).transpose(1, 0, 2),
        "tok",
        split_axis=0,
        concat_axis=0,
        tiled=True,
    )
    key_flat, value_half, qk_rows, v_rows = lax.optimization_barrier(
        (key_rot.reshape(tok_rows, width_dev), value_half, qk_rows, v_rows)
    )
    sent_keys, sent_values = [
        lax.all_to_all(
            select_rows(slot_hits, rows).reshape(shards, chunk, width_dev),
            "tok",
            split_axis=0,
            concat_axis=0,
            tiled=True,
        )
        for rows in (key_flat, value_half)
    ]
    cache_hits = slot_target[None, :] == local[:, None]
    cache_keys = select_rows(cache_hits, sent_keys.reshape(tok_rows, width_dev))
    cache_values = select_rows(cache_hits, sent_values.reshape(tok_rows, width_dev))

    attended = attend_head(starts, target[:, None, :], qk_rows, v_rows)
    attended = lax.all_to_all(
        attended.reshape(shards, tok_rows, head_size),
        "tok",
        split_axis=0,
        concat_axis=0,
        tiled=True,
    )
    attended = attended.transpose(1, 0, 2).reshape(tok_rows, width_dev)
    mixed_rows = (
        lax.psum_scatter(
            lax.dot_general(
                w_out, attended, (((0,), (1,)), ((), ())), preferred_element_type=jnp.float32
            ).astype(jnp.bfloat16),
            "rep",
            scatter_dimension=0,
            tiled=True,
        )
        .astype(jnp.float32)
        .T
    )
    mixed_sums = lax.psum(jnp.sum(mixed_rows * mixed_rows, axis=1), "rep")
    normed_rows = (
        mixed_rows * lax.rsqrt(mixed_sums / full_width + EPSILON)[:, None] * post_gain[None, :]
    )
    output = (packed_hidden.astype(jnp.float32) + normed_rows).astype(jnp.bfloat16)
    return (output, cache_keys, cache_values)


def solution(mesh):
    def pick(*operands):
        heads_dev = operands[0].shape[1] // HEAD_DIM
        chosen = body_heads if heads_dev == mesh.shape["tok"] else body
        return chosen(*operands)

    return jax.shard_map(
        pick,
        mesh=mesh,
        in_specs=(
            P("tok", "rep"),
            P(None, "rep"),
            P(None, "rep"),
            P(None, "rep"),
            P("rep", None),
            P("rep"),
            P("rep"),
            P("rep"),
            P(),
            P(),
            P(),
            P(),
            P(),
        ),
        out_specs=(P("tok", "rep"), P("tok", "rep"), P("tok", "rep")),
        check_vma=False,
    )
```

```python
import functools
import math

import jax
import jax.numpy as jnp
from jax import lax
from jax.experimental import pallas as pl
from jax.experimental.pallas import tpu as pltpu
from jax.sharding import PartitionSpec as P

HEAD_DIM = 128


EPSILON = 1e-06
ROPE_BASE = 500000.0


def rotate(values, positions):
    half_size = values.shape[-1] // 2
    frequency = ROPE_BASE ** (-jnp.arange(half_size, dtype=jnp.float32) * 2.0 / values.shape[-1])
    angles = positions.astype(jnp.float32)[:, None] * frequency[None, :]
    cosine = jnp.cos(angles)[:, None, :]
    sine_part = jnp.sin(angles)[:, None, :]
    lower_half = values[..., :half_size]
    upper_half = values[..., half_size:]
    return jnp.concatenate(
        [
            lower_half * cosine - upper_half * sine_part,
            upper_half * cosine + lower_half * sine_part,
        ],
        axis=-1,
    )


def bucketed(table_rows, row_order, shards):
    picked = table_rows[row_order]
    return picked.reshape(shards, picked.shape[0] // shards, picked.shape[1])


def placement_order(sources, shard_rows):
    local_ids = jnp.arange(sources.shape[0], dtype=jnp.int32)
    arrival = jnp.argsort(sources * shard_rows + local_ids)
    return jnp.argsort(arrival)


def body(
    hidden_in,
    w_query,
    w_key,
    w_value,
    w_out,
    q_gain,
    k_gain,
    post_gain,
    prompt_lengths,
    segment_ids,
    deal,
    inverse,
    slots,
):
    tok_rows, width_dev = hidden_in.shape
    full_width = w_query.shape[0]
    head_size = HEAD_DIM
    heads_dev = width_dev // head_size
    shards = lax.axis_size("tok")
    first_row = lax.axis_index("tok") * tok_rows
    my_packed = lax.dynamic_slice_in_dim(deal, first_row, tok_rows)
    my_segment = segment_ids[my_packed]
    prompt_ids = jnp.arange(prompt_lengths.shape[0], dtype=jnp.int32)
    prompt_starts = jnp.cumsum(prompt_lengths) - prompt_lengths
    my_start = jnp.sum(
        jnp.where(my_segment[:, None] == prompt_ids[None, :], prompt_starts[None, :], 0), axis=1
    )
    positions = my_packed - my_start
    pieces = lax.all_gather(hidden_in, "rep", axis=1, tiled=True)
    query_rows = jnp.dot(pieces, w_query, preferred_element_type=jnp.float32)
    key_rows = jnp.dot(pieces, w_key, preferred_element_type=jnp.float32)
    value_rows = jnp.dot(pieces, w_value, preferred_element_type=jnp.float32)
    query_sums, key_sums = lax.psum(
        (jnp.sum(query_rows * query_rows, axis=1), jnp.sum(key_rows * key_rows, axis=1)), "rep"
    )
    query_rows = (
        query_rows * lax.rsqrt(query_sums / full_width + EPSILON)[:, None] * q_gain[None, :]
    )
    key_rows = key_rows * lax.rsqrt(key_sums / full_width + EPSILON)[:, None] * k_gain[None, :]
    query_rot = rotate(query_rows.reshape(tok_rows, heads_dev, head_size), positions).astype(
        jnp.bfloat16
    )
    key_rot = (
        rotate(key_rows.reshape(tok_rows, heads_dev, head_size), positions)
        .astype(jnp.bfloat16)
        .reshape(tok_rows, width_dev)
    )
    value_half = value_rows.astype(jnp.bfloat16)
    scale = head_size ** (-0.5)

    def attend(state_now, key_block, value_block, key_packed):
        row_top, totals, weighted = state_now
        block_keys = key_block.reshape(key_block.shape[0], heads_dev, head_size)
        block_values = value_block.reshape(value_block.shape[0], heads_dev, head_size)
        key_segment = segment_ids[key_packed]
        allowed = (key_segment[None, :] == my_segment[:, None]) & (
            key_packed[None, :] <= my_packed[:, None]
        )
        scores = (
            jnp.einsum("qhd,khd->hqk", query_rot, block_keys, preferred_element_type=jnp.float32)
            * scale
        )
        masked = jnp.where(allowed[None], scores, -1e30)
        new_top = jnp.maximum(row_top, jnp.max(masked, axis=2))
        weights = jnp.where(allowed[None], jnp.exp(masked - new_top[:, :, None]), 0.0)
        factor = jnp.exp(row_top - new_top)
        totals = totals * factor + jnp.sum(weights, axis=2)
        weighted = weighted * factor[:, :, None] + jnp.einsum(
            "hqk,khd->hqd",
            weights.astype(jnp.bfloat16),
            block_values,
            preferred_element_type=jnp.float32,
        )
        return (new_top, totals, weighted)

    start_state = (
        jnp.full((heads_dev, tok_rows), -1e30, jnp.float32),
        jnp.zeros((heads_dev, tok_rows), jnp.float32),
        jnp.zeros((heads_dev, tok_rows, head_size), jnp.float32),
    )
    owned_rows = lax.dynamic_slice_in_dim(jnp.argsort(slots), first_row, tok_rows)
    my_slots = lax.dynamic_slice_in_dim(slots, first_row, tok_rows)
    slot_order = jnp.argsort(my_slots)
    sent_keys, sent_values = (
        lax.all_to_all(
            bucketed(key_rot, slot_order, shards), "tok", split_axis=0, concat_axis=0, tiled=True
        ),
        lax.all_to_all(
            bucketed(value_half, slot_order, shards), "tok", split_axis=0, concat_axis=0, tiled=True
        ),
    )
    arrival = placement_order(owned_rows // tok_rows, tok_rows)
    cache_keys = sent_keys.reshape(tok_rows, width_dev)[arrival]
    cache_values = sent_values.reshape(tok_rows, width_dev)[arrival]
    pieces = (
        lax.all_gather(key_rot, "tok", axis=0, tiled=True),
        lax.all_gather(value_half, "tok", axis=0, tiled=True),
    )
    key_all = pieces[0]
    block_size = math.gcd(key_all.shape[0], tok_rows)
    block_count = key_all.shape[0] // block_size

    def advance(state_in, block_set):
        return (attend(state_in, block_set[0], block_set[1], block_set[2]), None)

    state_out, _ = lax.scan(
        advance,
        start_state,
        (
            key_all.reshape(block_count, block_size, width_dev),
            pieces[1].reshape(block_count, block_size, width_dev),
            deal.reshape(block_count, block_size),
        ),
    )
    row_top, totals, weighted = state_out
    attended = (
        (weighted / totals[:, :, None])
        .transpose(1, 0, 2)
        .reshape(tok_rows, width_dev)
        .astype(jnp.bfloat16)
    )
    mixed_rows = (
        lax.psum_scatter(
            lax.dot_general(
                w_out, attended, (((0,), (1,)), ((), ())), preferred_element_type=jnp.float32
            ).astype(jnp.bfloat16),
            "rep",
            scatter_dimension=0,
            tiled=True,
        )
        .astype(jnp.float32)
        .T
    )
    mixed_sums = lax.psum(jnp.sum(mixed_rows * mixed_rows, axis=1), "rep")
    normed_rows = (
        mixed_rows * lax.rsqrt(mixed_sums / full_width + EPSILON)[:, None] * post_gain[None, :]
    )
    result_rows = (hidden_in.astype(jnp.float32) + normed_rows).astype(jnp.bfloat16)
    packed_order = jnp.argsort(my_packed)
    returned = lax.all_to_all(
        bucketed(result_rows, packed_order, shards), "tok", split_axis=0, concat_axis=0, tiled=True
    )
    my_dealt = lax.dynamic_slice_in_dim(inverse, first_row, tok_rows)
    output = returned.reshape(tok_rows, width_dev)[placement_order(my_dealt // tok_rows, tok_rows)]
    return (output, cache_keys, cache_values)


def select_rows(hits, rows):
    return jnp.dot(
        hits.astype(jnp.bfloat16), rows, preferred_element_type=jnp.float32
    ).astype(jnp.bfloat16)


def attend_kernel(
    starts_ref, target_ref, qk_ref, v_ref, out_ref, keys, values, *, size, head_size, part, parts
):
    share = size // parts
    skip = part * share
    block = pl.program_id(0)
    mine = pl.ds(pl.multiple_of(block * size, size), size)
    row_iota = lax.broadcasted_iota(jnp.int32, (size, size), 0)
    hits = jnp.where(row_iota == target_ref[0], 1.0, 0.0).astype(jnp.bfloat16)
    qk_rows = qk_ref[...].reshape(size, 2 * head_size)
    v_rows = v_ref[...].reshape(size, head_size)
    packed_qk = jnp.dot(hits, qk_rows, preferred_element_type=jnp.float32).astype(jnp.bfloat16)
    packed_v = jnp.dot(hits, v_rows, preferred_element_type=jnp.float32).astype(jnp.bfloat16)
    query = packed_qk[skip : skip + share, :head_size]
    keys[mine, :] = packed_qk[:, head_size:]
    values[mine, :] = packed_v
    base_row = block * size
    first = base_row + skip
    rows = first + lax.broadcasted_iota(jnp.int32, (share, 1), 0)
    row_start = jnp.zeros((share, 1), jnp.int32)
    low = jnp.int32(0)
    for prompt in range(starts_ref.shape[0]):
        start = starts_ref[prompt]
        row_start = jnp.where(rows >= start, jnp.maximum(row_start, start), row_start)
        low = jnp.where(first >= start, jnp.maximum(low, start), low)
    scale = head_size ** (-0.5) * math.log2(math.e)

    def scores_of(key_rows):
        return lax.dot_general(
            query, key_rows, (((1,), (1,)), ((), ())), preferred_element_type=jnp.float32
        ) * scale

    column_iota = lax.broadcasted_iota(jnp.int32, (share, size), 1)
    row_iota = lax.broadcasted_iota(jnp.int32, (share, size), 0)
    allowed = (column_iota >= row_start - base_row) & (column_iota <= row_iota + skip)
    scores = jnp.where(allowed, scores_of(packed_qk[:, head_size:]), -1e30)
    top = jnp.max(scores, axis=1, keepdims=True)
    weights = jnp.exp2(scores - top)
    totals = jnp.sum(weights, axis=1, keepdims=True)
    weighted = jnp.dot(
        weights.astype(jnp.bfloat16), packed_v, preferred_element_type=jnp.float32
    )

    def earlier(step, state):
        top, totals, weighted = state
        base = pl.multiple_of((block - 1 - step) * size, size)
        scores = scores_of(keys[pl.ds(base, size), :])
        scores = jnp.where(column_iota >= row_start - base, scores, -1e30)
        new_top = jnp.maximum(top, jnp.max(scores, axis=1, keepdims=True))
        factor = jnp.exp2(top - new_top)
        weights = jnp.exp2(scores - new_top)
        totals = totals * factor + jnp.sum(weights, axis=1, keepdims=True)
        weighted = weighted * factor + jnp.dot(
            weights.astype(jnp.bfloat16),
            values[pl.ds(base, size), :],
            preferred_element_type=jnp.float32,
        )
        return (new_top, totals, weighted)

    top, totals, weighted = lax.fori_loop(
        0, block - low // size, earlier, (top, totals, weighted)
    )
    out_ref[...] = (weighted / totals).astype(jnp.bfloat16)


def attend_head(starts, target, qk_rows, v_rows, part, parts):
    shards, tok_rows, head_size = v_rows.shape
    chunk = tok_rows // shards
    return pl.pallas_call(
        functools.partial(
            attend_kernel, size=tok_rows, head_size=head_size, part=part, parts=parts
        ),
        out_shape=jax.ShapeDtypeStruct((shards * tok_rows // parts, head_size), jnp.bfloat16),
        grid_spec=pltpu.PrefetchScalarGridSpec(
            num_scalar_prefetch=1,
            grid=(shards,),
            in_specs=[
                pl.BlockSpec((1, 1, tok_rows), lambda i, s: (i, 0, 0)),
                pl.BlockSpec((shards, chunk, 2 * head_size), lambda i, s: (0, i, 0)),
                pl.BlockSpec((shards, chunk, head_size), lambda i, s: (0, i, 0)),
            ],
            out_specs=pl.BlockSpec((tok_rows // parts, head_size), lambda i, s: (i, 0)),
            scratch_shapes=[
                pltpu.VMEM((shards * tok_rows, head_size), jnp.bfloat16),
                pltpu.VMEM((shards * tok_rows, head_size), jnp.bfloat16),
            ],
        ),
        compiler_params=pltpu.CompilerParams(
            dimension_semantics=("arbitrary",), vmem_limit_bytes=48 << 20
        ),
        cost_estimate=pl.CostEstimate(
            flops=8 * tok_rows * tok_rows * shards * head_size * 3 // parts,
            bytes_accessed=8 * shards * tok_rows * head_size,
            transcendentals=3 * shards * tok_rows * tok_rows,
        ),
    )(starts, target, qk_rows, v_rows)


def rope_kernel(q_ref, k_ref, q_scale, k_scale, q_gain, k_gain, cosine, sine, qk_ref, key_ref):
    head_size = q_ref.shape[1]

    def turned(rows, scale, gain):
        normed = rows[...] * scale[...] * gain[...]
        other = pltpu.roll(normed, head_size // 2, 1)
        return (normed * cosine[...] + other * sine[...]).astype(jnp.bfloat16)

    qk_ref[0, :, :head_size] = turned(q_ref, q_scale, q_gain)
    key_rows = turned(k_ref, k_scale, k_gain)
    qk_ref[0, :, head_size:] = key_rows
    key_ref[...] = key_rows


def rope_heads(query_rows, key_rows, q_scale, k_scale, q_gain, k_gain, cosine, sine):
    rows, width = query_rows.shape
    head_size = cosine.shape[1]
    heads = width // head_size
    wide = pl.BlockSpec((rows, head_size), lambda h: (0, h))
    thin = pl.BlockSpec((rows, 1), lambda h: (0, 0))
    gain = pl.BlockSpec((1, head_size), lambda h: (0, h))
    table = pl.BlockSpec((rows, head_size), lambda h: (0, 0))
    return pl.pallas_call(
        rope_kernel,
        out_shape=(
            jax.ShapeDtypeStruct((heads, rows, 2 * head_size), jnp.bfloat16),
            jax.ShapeDtypeStruct((rows, width), jnp.bfloat16),
        ),
        grid=(heads,),
        in_specs=[wide, wide, thin, thin, gain, gain, table, table],
        out_specs=(pl.BlockSpec((1, rows, 2 * head_size), lambda h: (h, 0, 0)), wide),
        compiler_params=pltpu.CompilerParams(vmem_limit_bytes=24 << 20),
        cost_estimate=pl.CostEstimate(
            flops=14 * rows * width, bytes_accessed=14 * rows * width, transcendentals=0
        ),
    )(query_rows, key_rows, q_scale, k_scale, q_gain, k_gain, cosine, sine)


def value_kernel(x_ref, w_ref, flat_ref, heads_ref):
    rows = jnp.dot(x_ref[...], w_ref[...], preferred_element_type=jnp.float32).astype(
        jnp.bfloat16
    )
    flat_ref[...] = rows
    count, _, head_size = heads_ref.shape
    for head in range(count):
        heads_ref[head] = rows[:, head * head_size : (head + 1) * head_size]


def value_heads(pieces, w_value, head_size):
    rows, depth = pieces.shape
    width = w_value.shape[1]
    count = 2
    return pl.pallas_call(
        value_kernel,
        out_shape=(
            jax.ShapeDtypeStruct((rows, width), jnp.bfloat16),
            jax.ShapeDtypeStruct((width // head_size, rows, head_size), jnp.bfloat16),
        ),
        grid=(width // (count * head_size),),
        in_specs=[
            pl.BlockSpec((rows, depth), lambda h: (0, 0)),
            pl.BlockSpec((depth, count * head_size), lambda h: (0, h)),
        ],
        out_specs=(
            pl.BlockSpec((rows, count * head_size), lambda h: (0, h)),
            pl.BlockSpec((count, rows, head_size), lambda h: (h, 0, 0)),
        ),
        compiler_params=pltpu.CompilerParams(vmem_limit_bytes=40 << 20),
        cost_estimate=pl.CostEstimate(
            flops=2 * rows * depth * width,
            bytes_accessed=2 * (rows * depth + depth * width + 2 * rows * width),
            transcendentals=0,
        ),
    )(pieces, w_value)


def body_heads(
    hidden_in,
    w_query,
    w_key,
    w_value,
    w_out,
    q_gain,
    k_gain,
    post_gain,
    prompt_lengths,
    segment_ids,
    deal,
    inverse,
    slots,
):
    tok_rows, width_dev = hidden_in.shape
    full_width = w_query.shape[0]
    head_size = HEAD_DIM
    heads_dev = width_dev // head_size
    shards = lax.axis_size("tok")
    chunk = tok_rows // shards
    me = lax.axis_index("tok")
    first_row = me * tok_rows
    pieces = lax.all_gather(hidden_in, "rep", axis=1, tiled=True)

    local = jnp.arange(tok_rows, dtype=jnp.int32)
    starts = jnp.cumsum(prompt_lengths) - prompt_lengths
    my_packed = lax.dynamic_slice_in_dim(deal, first_row, tok_rows)
    my_slots = lax.dynamic_slice_in_dim(slots, first_row, tok_rows)
    rank = jnp.sum((my_packed[None, :] < my_packed[:, None]).astype(jnp.int32), axis=1)
    sort_hits = rank[None, :] == local[:, None]
    sorted_packed = jnp.sum(jnp.where(sort_hits, my_packed[None, :], 0), axis=1)
    sorted_slots = jnp.sum(jnp.where(sort_hits, my_slots[None, :], 0), axis=1)
    my_start = jnp.max(
        jnp.where(starts[None, :] <= sorted_packed[:, None], starts[None, :], 0), axis=1
    )
    positions = sorted_packed - my_start

    source = inverse.reshape(shards, tok_rows) // tok_rows
    before = (source[:, None, :] == source[:, :, None]) & (local[None, None, :] < local[None, :, None])
    arrived = source * chunk + jnp.sum(before.astype(jnp.int32), axis=2)
    target = jnp.sum(
        jnp.where(arrived[:, :, None] == local[None, None, :], local[None, :, None], 0), axis=1
    )

    slot_rank = jnp.sum((sorted_slots[None, :] < sorted_slots[:, None]).astype(jnp.int32), axis=1)
    slot_hits = slot_rank[None, :] == local[:, None]
    slot_rows = slots.reshape(shards, tok_rows) - first_row
    owned = (slot_rows >= 0) & (slot_rows < tok_rows)
    ahead = owned[:, None, :] & (slot_rows[:, None, :] < slot_rows[:, :, None])
    landed = jnp.arange(shards, dtype=jnp.int32)[:, None] * chunk + jnp.sum(
        ahead.astype(jnp.int32), axis=2
    )
    landed = jnp.where(owned, landed, -1).reshape(-1)
    slot_target = jnp.sum(
        jnp.where(landed[:, None] == local[None, :], slot_rows.reshape(-1)[:, None], 0), axis=0
    )

    sent_hidden = lax.all_to_all(
        select_rows(sort_hits, hidden_in).reshape(shards, chunk, width_dev),
        "tok",
        split_axis=0,
        concat_axis=0,
        tiled=True,
    )
    half_size = head_size // 2
    frequency = ROPE_BASE ** (-jnp.arange(half_size, dtype=jnp.float32) * 2.0 / head_size)
    angles = positions.astype(jnp.float32)[:, None] * frequency[None, :]
    cosine, sine = jnp.cos(angles), jnp.sin(angles)
    cosine = jnp.concatenate([cosine, cosine], axis=1)
    sine = jnp.concatenate([-sine, sine], axis=1)
    pieces, sent_hidden, cosine, sine, target, slot_target = lax.optimization_barrier(
        (pieces, sent_hidden, cosine, sine, target, slot_target)
    )
    my_target = lax.dynamic_index_in_dim(target, me, 0, keepdims=False)
    my_hits = my_target[None, :] == local[:, None]

    pieces = select_rows(sort_hits, pieces)
    value_half, value_sent = value_heads(pieces, w_value, head_size)

    def exchange(rows):
        return lax.all_to_all(rows, "tok", split_axis=0, concat_axis=0, tiled=True)

    v_rows = exchange(value_sent)
    pieces, value_half = lax.optimization_barrier((pieces, value_half))
    query_rows = jnp.dot(pieces, w_query, preferred_element_type=jnp.float32)
    key_rows = jnp.dot(pieces, w_key, preferred_element_type=jnp.float32)
    sums = jnp.stack(
        [jnp.sum(query_rows * query_rows, axis=1), jnp.sum(key_rows * key_rows, axis=1)]
    )
    scales = lax.rsqrt(lax.psum(sums, "rep") / full_width + EPSILON)
    qk_sent, key_flat = rope_heads(
        query_rows,
        key_rows,
        scales[0][:, None],
        scales[1][:, None],
        q_gain[None, :],
        k_gain[None, :],
        cosine,
        sine,
    )
    qk_rows = exchange(qk_sent)
    qk_rows, v_rows, sent_hidden = lax.optimization_barrier((qk_rows, v_rows, sent_hidden))
    packed_hidden = select_rows(my_hits, sent_hidden.reshape(tok_rows, width_dev))

    parts = 2
    share = tok_rows // parts
    heads_out = [
        attend_head(starts, target[:, None, :], qk_rows, v_rows, part, parts).reshape(
            shards, share, head_size
        )
        for part in range(parts)
    ]
    first, last = lax.optimization_barrier((exchange(heads_out[0]), heads_out[1]))
    attended = [first, exchange(last)]
    attended[-1], key_flat, value_half = lax.optimization_barrier(
        (attended[-1], key_flat, value_half)
    )
    mixed = []
    for rows in attended:
        rows = rows.transpose(1, 0, 2).reshape(share, width_dev)
        mixed.append(
            lax.psum_scatter(
                lax.dot_general(
                    w_out, rows, (((0,), (1,)), ((), ())), preferred_element_type=jnp.float32
                ).astype(jnp.bfloat16),
                "rep",
                scatter_dimension=0,
                tiled=True,
            )
        )
    cache_hits = slot_target[None, :] == local[:, None]
    cache_keys, cache_values = [
        select_rows(
            cache_hits,
            exchange(select_rows(slot_hits, rows).reshape(shards, chunk, width_dev)).reshape(
                tok_rows, width_dev
            ),
        )
        for rows in (key_flat, value_half)
    ]
    mixed_rows = jnp.concatenate([rows.astype(jnp.float32).T for rows in mixed], axis=0)
    mixed_sums = lax.psum(jnp.sum(mixed_rows * mixed_rows, axis=1), "rep")
    normed_rows = (
        mixed_rows * lax.rsqrt(mixed_sums / full_width + EPSILON)[:, None] * post_gain[None, :]
    )
    output = (packed_hidden.astype(jnp.float32) + normed_rows).astype(jnp.bfloat16)
    return (output, cache_keys, cache_values)


def solution(mesh):
    def pick(*operands):
        heads_dev = operands[0].shape[1] // HEAD_DIM
        chosen = body_heads if heads_dev == mesh.shape["tok"] else body
        return chosen(*operands)

    return jax.shard_map(
        pick,
        mesh=mesh,
        in_specs=(
            P("tok", "rep"),
            P(None, "rep"),
            P(None, "rep"),
            P(None, "rep"),
            P("rep", None),
            P("rep"),
            P("rep"),
            P("rep"),
            P(),
            P(),
            P(),
            P(),
            P(),
        ),
        out_specs=(P("tok", "rep"), P("tok", "rep"), P("tok", "rep")),
        check_vma=False,
    )
```

```python
import functools
import math

import jax
import jax.numpy as jnp
from jax import lax
from jax.experimental import pallas as pl
from jax.experimental.pallas import tpu as pltpu
from jax.sharding import PartitionSpec as P

HEAD_DIM = 128


EPSILON = 1e-06
ROPE_BASE = 500000.0


def rotate(values, positions):
    half_size = values.shape[-1] // 2
    frequency = ROPE_BASE ** (-jnp.arange(half_size, dtype=jnp.float32) * 2.0 / values.shape[-1])
    angles = positions.astype(jnp.float32)[:, None] * frequency[None, :]
    cosine = jnp.cos(angles)[:, None, :]
    sine_part = jnp.sin(angles)[:, None, :]
    lower_half = values[..., :half_size]
    upper_half = values[..., half_size:]
    return jnp.concatenate(
        [
            lower_half * cosine - upper_half * sine_part,
            upper_half * cosine + lower_half * sine_part,
        ],
        axis=-1,
    )


def bucketed(table_rows, row_order, shards):
    picked = table_rows[row_order]
    return picked.reshape(shards, picked.shape[0] // shards, picked.shape[1])


def placement_order(sources, shard_rows):
    local_ids = jnp.arange(sources.shape[0], dtype=jnp.int32)
    arrival = jnp.argsort(sources * shard_rows + local_ids)
    return jnp.argsort(arrival)


def body(
    hidden_in,
    w_query,
    w_key,
    w_value,
    w_out,
    q_gain,
    k_gain,
    post_gain,
    prompt_lengths,
    segment_ids,
    deal,
    inverse,
    slots,
):
    tok_rows, width_dev = hidden_in.shape
    full_width = w_query.shape[0]
    head_size = HEAD_DIM
    heads_dev = width_dev // head_size
    shards = lax.axis_size("tok")
    first_row = lax.axis_index("tok") * tok_rows
    my_packed = lax.dynamic_slice_in_dim(deal, first_row, tok_rows)
    my_segment = segment_ids[my_packed]
    prompt_ids = jnp.arange(prompt_lengths.shape[0], dtype=jnp.int32)
    prompt_starts = jnp.cumsum(prompt_lengths) - prompt_lengths
    my_start = jnp.sum(
        jnp.where(my_segment[:, None] == prompt_ids[None, :], prompt_starts[None, :], 0), axis=1
    )
    positions = my_packed - my_start
    pieces = lax.all_gather(hidden_in, "rep", axis=1, tiled=True)
    query_rows = jnp.dot(pieces, w_query, preferred_element_type=jnp.float32)
    key_rows = jnp.dot(pieces, w_key, preferred_element_type=jnp.float32)
    value_rows = jnp.dot(pieces, w_value, preferred_element_type=jnp.float32)
    query_sums, key_sums = lax.psum(
        (jnp.sum(query_rows * query_rows, axis=1), jnp.sum(key_rows * key_rows, axis=1)), "rep"
    )
    query_rows = (
        query_rows * lax.rsqrt(query_sums / full_width + EPSILON)[:, None] * q_gain[None, :]
    )
    key_rows = key_rows * lax.rsqrt(key_sums / full_width + EPSILON)[:, None] * k_gain[None, :]
    query_rot = rotate(query_rows.reshape(tok_rows, heads_dev, head_size), positions).astype(
        jnp.bfloat16
    )
    key_rot = (
        rotate(key_rows.reshape(tok_rows, heads_dev, head_size), positions)
        .astype(jnp.bfloat16)
        .reshape(tok_rows, width_dev)
    )
    value_half = value_rows.astype(jnp.bfloat16)
    scale = head_size ** (-0.5)

    def attend(state_now, key_block, value_block, key_packed):
        row_top, totals, weighted = state_now
        block_keys = key_block.reshape(key_block.shape[0], heads_dev, head_size)
        block_values = value_block.reshape(value_block.shape[0], heads_dev, head_size)
        key_segment = segment_ids[key_packed]
        allowed = (key_segment[None, :] == my_segment[:, None]) & (
            key_packed[None, :] <= my_packed[:, None]
        )
        scores = (
            jnp.einsum("qhd,khd->hqk", query_rot, block_keys, preferred_element_type=jnp.float32)
            * scale
        )
        masked = jnp.where(allowed[None], scores, -1e30)
        new_top = jnp.maximum(row_top, jnp.max(masked, axis=2))
        weights = jnp.where(allowed[None], jnp.exp(masked - new_top[:, :, None]), 0.0)
        factor = jnp.exp(row_top - new_top)
        totals = totals * factor + jnp.sum(weights, axis=2)
        weighted = weighted * factor[:, :, None] + jnp.einsum(
            "hqk,khd->hqd",
            weights.astype(jnp.bfloat16),
            block_values,
            preferred_element_type=jnp.float32,
        )
        return (new_top, totals, weighted)

    start_state = (
        jnp.full((heads_dev, tok_rows), -1e30, jnp.float32),
        jnp.zeros((heads_dev, tok_rows), jnp.float32),
        jnp.zeros((heads_dev, tok_rows, head_size), jnp.float32),
    )
    owned_rows = lax.dynamic_slice_in_dim(jnp.argsort(slots), first_row, tok_rows)
    my_slots = lax.dynamic_slice_in_dim(slots, first_row, tok_rows)
    slot_order = jnp.argsort(my_slots)
    sent_keys, sent_values = (
        lax.all_to_all(
            bucketed(key_rot, slot_order, shards), "tok", split_axis=0, concat_axis=0, tiled=True
        ),
        lax.all_to_all(
            bucketed(value_half, slot_order, shards), "tok", split_axis=0, concat_axis=0, tiled=True
        ),
    )
    arrival = placement_order(owned_rows // tok_rows, tok_rows)
    cache_keys = sent_keys.reshape(tok_rows, width_dev)[arrival]
    cache_values = sent_values.reshape(tok_rows, width_dev)[arrival]
    pieces = (
        lax.all_gather(key_rot, "tok", axis=0, tiled=True),
        lax.all_gather(value_half, "tok", axis=0, tiled=True),
    )
    key_all = pieces[0]
    block_size = math.gcd(key_all.shape[0], tok_rows)
    block_count = key_all.shape[0] // block_size

    def advance(state_in, block_set):
        return (attend(state_in, block_set[0], block_set[1], block_set[2]), None)

    state_out, _ = lax.scan(
        advance,
        start_state,
        (
            key_all.reshape(block_count, block_size, width_dev),
            pieces[1].reshape(block_count, block_size, width_dev),
            deal.reshape(block_count, block_size),
        ),
    )
    row_top, totals, weighted = state_out
    attended = (
        (weighted / totals[:, :, None])
        .transpose(1, 0, 2)
        .reshape(tok_rows, width_dev)
        .astype(jnp.bfloat16)
    )
    mixed_rows = (
        lax.psum_scatter(
            lax.dot_general(
                w_out, attended, (((0,), (1,)), ((), ())), preferred_element_type=jnp.float32
            ).astype(jnp.bfloat16),
            "rep",
            scatter_dimension=0,
            tiled=True,
        )
        .astype(jnp.float32)
        .T
    )
    mixed_sums = lax.psum(jnp.sum(mixed_rows * mixed_rows, axis=1), "rep")
    normed_rows = (
        mixed_rows * lax.rsqrt(mixed_sums / full_width + EPSILON)[:, None] * post_gain[None, :]
    )
    result_rows = (hidden_in.astype(jnp.float32) + normed_rows).astype(jnp.bfloat16)
    packed_order = jnp.argsort(my_packed)
    returned = lax.all_to_all(
        bucketed(result_rows, packed_order, shards), "tok", split_axis=0, concat_axis=0, tiled=True
    )
    my_dealt = lax.dynamic_slice_in_dim(inverse, first_row, tok_rows)
    output = returned.reshape(tok_rows, width_dev)[placement_order(my_dealt // tok_rows, tok_rows)]
    return (output, cache_keys, cache_values)


def select_rows(hits, rows):
    return jnp.dot(
        hits.astype(jnp.bfloat16), rows, preferred_element_type=jnp.float32
    ).astype(jnp.bfloat16)


def attend_kernel(
    starts_ref, target_ref, qk_ref, v_ref, out_ref, keys, values, *, size, head_size, part, parts
):
    share = size // parts
    skip = part * share
    block = pl.program_id(0)
    mine = pl.ds(pl.multiple_of(block * size, size), size)
    row_iota = lax.broadcasted_iota(jnp.int32, (size, size), 0)
    hits = jnp.where(row_iota == target_ref[0], 1.0, 0.0).astype(jnp.bfloat16)
    qk_rows = qk_ref[...].reshape(size, 2 * head_size)
    v_rows = v_ref[...].reshape(size, head_size)
    packed_qk = jnp.dot(hits, qk_rows, preferred_element_type=jnp.float32).astype(jnp.bfloat16)
    packed_v = jnp.dot(hits, v_rows, preferred_element_type=jnp.float32).astype(jnp.bfloat16)
    query = packed_qk[skip : skip + share, :head_size]
    keys[mine, :] = packed_qk[:, head_size:]
    values[mine, :] = packed_v
    base_row = block * size
    first = base_row + skip
    rows = first + lax.broadcasted_iota(jnp.int32, (share, 1), 0)
    row_start = jnp.zeros((share, 1), jnp.int32)
    low = jnp.int32(0)
    for prompt in range(starts_ref.shape[0]):
        start = starts_ref[prompt]
        row_start = jnp.where(rows >= start, jnp.maximum(row_start, start), row_start)
        low = jnp.where(first >= start, jnp.maximum(low, start), low)
    scale = head_size ** (-0.5) * math.log2(math.e)

    def scores_of(key_rows):
        return lax.dot_general(
            query, key_rows, (((1,), (1,)), ((), ())), preferred_element_type=jnp.float32
        ) * scale

    column_iota = lax.broadcasted_iota(jnp.int32, (share, size), 1)
    row_iota = lax.broadcasted_iota(jnp.int32, (share, size), 0)
    allowed = (column_iota >= row_start - base_row) & (column_iota <= row_iota + skip)
    scores = jnp.where(allowed, scores_of(packed_qk[:, head_size:]), -1e30)
    top = jnp.max(scores, axis=1, keepdims=True)
    weights = jnp.exp2(scores - top)
    totals = jnp.sum(weights, axis=1, keepdims=True)
    weighted = jnp.dot(
        weights.astype(jnp.bfloat16), packed_v, preferred_element_type=jnp.float32
    )

    def earlier(step, state):
        top, totals, weighted = state
        base = pl.multiple_of((block - 1 - step) * size, size)
        scores = scores_of(keys[pl.ds(base, size), :])
        scores = jnp.where(column_iota >= row_start - base, scores, -1e30)
        new_top = jnp.maximum(top, jnp.max(scores, axis=1, keepdims=True))
        factor = jnp.exp2(top - new_top)
        weights = jnp.exp2(scores - new_top)
        totals = totals * factor + jnp.sum(weights, axis=1, keepdims=True)
        weighted = weighted * factor + jnp.dot(
            weights.astype(jnp.bfloat16),
            values[pl.ds(base, size), :],
            preferred_element_type=jnp.float32,
        )
        return (new_top, totals, weighted)

    top, totals, weighted = lax.fori_loop(
        0, block - low // size, earlier, (top, totals, weighted)
    )
    out_ref[...] = (weighted / totals).astype(jnp.bfloat16)


def attend_head(starts, target, qk_rows, v_rows, part, parts):
    shards, tok_rows, head_size = v_rows.shape
    chunk = tok_rows // shards
    return pl.pallas_call(
        functools.partial(
            attend_kernel, size=tok_rows, head_size=head_size, part=part, parts=parts
        ),
        out_shape=jax.ShapeDtypeStruct((shards * tok_rows // parts, head_size), jnp.bfloat16),
        grid_spec=pltpu.PrefetchScalarGridSpec(
            num_scalar_prefetch=1,
            grid=(shards,),
            in_specs=[
                pl.BlockSpec((1, 1, tok_rows), lambda i, s: (i, 0, 0)),
                pl.BlockSpec((shards, chunk, 2 * head_size), lambda i, s: (0, i, 0)),
                pl.BlockSpec((shards, chunk, head_size), lambda i, s: (0, i, 0)),
            ],
            out_specs=pl.BlockSpec((tok_rows // parts, head_size), lambda i, s: (i, 0)),
            scratch_shapes=[
                pltpu.VMEM((shards * tok_rows, head_size), jnp.bfloat16),
                pltpu.VMEM((shards * tok_rows, head_size), jnp.bfloat16),
            ],
        ),
        compiler_params=pltpu.CompilerParams(
            dimension_semantics=("arbitrary",), vmem_limit_bytes=48 << 20
        ),
        cost_estimate=pl.CostEstimate(
            flops=8 * tok_rows * tok_rows * shards * head_size * 3 // parts,
            bytes_accessed=8 * shards * tok_rows * head_size,
            transcendentals=3 * shards * tok_rows * tok_rows,
        ),
    )(starts, target, qk_rows, v_rows)


def rope_kernel(q_ref, k_ref, q_scale, k_scale, q_gain, k_gain, cosine, sine, qk_ref, key_ref):
    head_size = q_ref.shape[1]

    def turned(rows, scale, gain):
        normed = rows[...] * scale[...] * gain[...]
        other = pltpu.roll(normed, head_size // 2, 1)
        return (normed * cosine[...] + other * sine[...]).astype(jnp.bfloat16)

    qk_ref[0, :, :head_size] = turned(q_ref, q_scale, q_gain)
    key_rows = turned(k_ref, k_scale, k_gain)
    qk_ref[0, :, head_size:] = key_rows
    key_ref[...] = key_rows


def rope_heads(query_rows, key_rows, q_scale, k_scale, q_gain, k_gain, cosine, sine):
    rows, width = query_rows.shape
    head_size = cosine.shape[1]
    heads = width // head_size
    wide = pl.BlockSpec((rows, head_size), lambda h: (0, h))
    thin = pl.BlockSpec((rows, 1), lambda h: (0, 0))
    gain = pl.BlockSpec((1, head_size), lambda h: (0, h))
    table = pl.BlockSpec((rows, head_size), lambda h: (0, 0))
    return pl.pallas_call(
        rope_kernel,
        out_shape=(
            jax.ShapeDtypeStruct((heads, rows, 2 * head_size), jnp.bfloat16),
            jax.ShapeDtypeStruct((rows, width), jnp.bfloat16),
        ),
        grid=(heads,),
        in_specs=[wide, wide, thin, thin, gain, gain, table, table],
        out_specs=(pl.BlockSpec((1, rows, 2 * head_size), lambda h: (h, 0, 0)), wide),
        compiler_params=pltpu.CompilerParams(vmem_limit_bytes=24 << 20),
        cost_estimate=pl.CostEstimate(
            flops=14 * rows * width, bytes_accessed=14 * rows * width, transcendentals=0
        ),
    )(query_rows, key_rows, q_scale, k_scale, q_gain, k_gain, cosine, sine)


def value_kernel(owner_ref, x_ref, w_ref, so_far_ref, flat_ref, heads_ref):
    rows = so_far_ref[...] + jnp.dot(x_ref[...], w_ref[...], preferred_element_type=jnp.float32)
    rows = rows.astype(jnp.bfloat16)
    flat_ref[...] = rows
    count, _, head_size = heads_ref.shape
    for head in range(count):
        heads_ref[head] = rows[:, head * head_size : (head + 1) * head_size]


def value_heads(owner, pieces, w_value, so_far, head_size):
    rows, depth = pieces.shape
    width = w_value.shape[1]
    count = 2
    return pl.pallas_call(
        value_kernel,
        out_shape=(
            jax.ShapeDtypeStruct((rows, width), jnp.bfloat16),
            jax.ShapeDtypeStruct((width // head_size, rows, head_size), jnp.bfloat16),
        ),
        grid_spec=pltpu.PrefetchScalarGridSpec(
            num_scalar_prefetch=1,
            grid=(width // (count * head_size),),
            in_specs=[
                pl.BlockSpec((rows, depth), lambda h, owner: (0, 0)),
                pl.BlockSpec((depth, count * head_size), lambda h, owner: (owner[0], h)),
                pl.BlockSpec((rows, count * head_size), lambda h, owner: (0, h)),
            ],
            out_specs=(
                pl.BlockSpec((rows, count * head_size), lambda h, owner: (0, h)),
                pl.BlockSpec((count, rows, head_size), lambda h, owner: (h, 0, 0)),
            ),
        ),
        compiler_params=pltpu.CompilerParams(vmem_limit_bytes=40 << 20),
        cost_estimate=pl.CostEstimate(
            flops=2 * rows * depth * width,
            bytes_accessed=2 * (rows * depth + depth * width + 2 * rows * width),
            transcendentals=0,
        ),
    )(owner, pieces, w_value, so_far)


def body_heads(
    hidden_in,
    w_query,
    w_key,
    w_value,
    w_out,
    q_gain,
    k_gain,
    post_gain,
    prompt_lengths,
    segment_ids,
    deal,
    inverse,
    slots,
):
    tok_rows, width_dev = hidden_in.shape
    full_width = w_query.shape[0]
    head_size = HEAD_DIM
    heads_dev = width_dev // head_size
    shards = lax.axis_size("tok")
    chunk = tok_rows // shards
    me = lax.axis_index("tok")
    first_row = me * tok_rows
    half_rows = tok_rows // 2
    corner = lax.axis_index("rep")
    across = [(i, i ^ 1) for i in range(4)]
    along = [(i, i ^ 2) for i in range(4)]

    local = jnp.arange(tok_rows, dtype=jnp.int32)
    starts = jnp.cumsum(prompt_lengths) - prompt_lengths
    my_packed = lax.dynamic_slice_in_dim(deal, first_row, tok_rows)
    my_slots = lax.dynamic_slice_in_dim(slots, first_row, tok_rows)
    rank = jnp.sum((my_packed[None, :] < my_packed[:, None]).astype(jnp.int32), axis=1)
    sort_hits = rank[None, :] == local[:, None]
    sorted_packed = jnp.sum(jnp.where(sort_hits, my_packed[None, :], 0), axis=1)
    sorted_slots = jnp.sum(jnp.where(sort_hits, my_slots[None, :], 0), axis=1)
    my_start = jnp.max(
        jnp.where(starts[None, :] <= sorted_packed[:, None], starts[None, :], 0), axis=1
    )
    positions = sorted_packed - my_start

    source = inverse.reshape(shards, tok_rows) // tok_rows
    before = (source[:, None, :] == source[:, :, None]) & (local[None, None, :] < local[None, :, None])
    arrived = source * chunk + jnp.sum(before.astype(jnp.int32), axis=2)
    target = jnp.sum(
        jnp.where(arrived[:, :, None] == local[None, None, :], local[None, :, None], 0), axis=1
    )

    slot_rank = jnp.sum((sorted_slots[None, :] < sorted_slots[:, None]).astype(jnp.int32), axis=1)
    slot_hits = slot_rank[None, :] == local[:, None]
    slot_rows = slots.reshape(shards, tok_rows) - first_row
    owned = (slot_rows >= 0) & (slot_rows < tok_rows)
    ahead = owned[:, None, :] & (slot_rows[:, None, :] < slot_rows[:, :, None])
    landed = jnp.arange(shards, dtype=jnp.int32)[:, None] * chunk + jnp.sum(
        ahead.astype(jnp.int32), axis=2
    )
    landed = jnp.where(owned, landed, -1).reshape(-1)
    slot_target = jnp.sum(
        jnp.where(landed[:, None] == local[None, :], slot_rows.reshape(-1)[:, None], 0), axis=0
    )

    piece = select_rows(sort_hits, hidden_in)
    piece_x = lax.ppermute(piece, "rep", across)
    piece_y = lax.ppermute(piece, "rep", along)
    piece_xy = jnp.concatenate(
        [
            lax.ppermute(piece_y[:half_rows], "rep", across),
            lax.ppermute(piece_x[half_rows:], "rep", along),
        ],
        axis=0,
    )

    def product(rows, weights, step):
        owned = lax.dynamic_slice_in_dim(weights, (corner ^ step) * width_dev, width_dev, axis=0)
        return jnp.dot(rows, owned, preferred_element_type=jnp.float32)

    sums_now = [product(piece, weights, 0) for weights in (w_value, w_query, w_key)]
    for step, rows in ((1, piece_x), (2, piece_y)):
        sums_now = [
            done + product(rows, weights, step)
            for done, weights in zip(sums_now, (w_value, w_query, w_key))
        ]

    sent_hidden = lax.all_to_all(
        piece.reshape(shards, chunk, width_dev),
        "tok",
        split_axis=0,
        concat_axis=0,
        tiled=True,
    )
    half_size = head_size // 2
    frequency = ROPE_BASE ** (-jnp.arange(half_size, dtype=jnp.float32) * 2.0 / head_size)
    angles = positions.astype(jnp.float32)[:, None] * frequency[None, :]
    cosine, sine = jnp.cos(angles), jnp.sin(angles)
    cosine = jnp.concatenate([cosine, cosine], axis=1)
    sine = jnp.concatenate([-sine, sine], axis=1)
    piece_xy, sent_hidden, cosine, sine, target, slot_target, sums_now = lax.optimization_barrier(
        (piece_xy, sent_hidden, cosine, sine, target, slot_target, sums_now)
    )
    my_target = lax.dynamic_index_in_dim(target, me, 0, keepdims=False)
    my_hits = my_target[None, :] == local[:, None]

    last = corner ^ 3
    value_half, value_sent = value_heads(last[None], piece_xy, w_value, sums_now[0], head_size)

    def exchange(rows):
        return lax.all_to_all(rows, "tok", split_axis=0, concat_axis=0, tiled=True)

    v_rows = exchange(value_sent)
    piece_xy, value_half = lax.optimization_barrier((piece_xy, value_half))
    query_rows = sums_now[1] + product(piece_xy, w_query, 3)
    key_rows = sums_now[2] + product(piece_xy, w_key, 3)
    sums = jnp.stack(
        [jnp.sum(query_rows * query_rows, axis=1), jnp.sum(key_rows * key_rows, axis=1)]
    )
    scales = lax.rsqrt(lax.psum(sums, "rep") / full_width + EPSILON)
    qk_sent, key_flat = rope_heads(
        query_rows,
        key_rows,
        scales[0][:, None],
        scales[1][:, None],
        q_gain[None, :],
        k_gain[None, :],
        cosine,
        sine,
    )
    qk_rows = exchange(qk_sent)
    qk_rows, v_rows, sent_hidden = lax.optimization_barrier((qk_rows, v_rows, sent_hidden))
    packed_hidden = select_rows(my_hits, sent_hidden.reshape(tok_rows, width_dev))

    parts = 2
    share = tok_rows // parts
    heads_out = [
        attend_head(starts, target[:, None, :], qk_rows, v_rows, part, parts).reshape(
            shards, share, head_size
        )
        for part in range(parts)
    ]
    first, last = lax.optimization_barrier((exchange(heads_out[0]), heads_out[1]))
    attended = [first, exchange(last)]
    attended[-1], key_flat, value_half = lax.optimization_barrier(
        (attended[-1], key_flat, value_half)
    )
    mixed = []
    for rows in attended:
        rows = rows.transpose(1, 0, 2).reshape(share, width_dev)
        mixed.append(
            lax.psum_scatter(
                lax.dot_general(
                    w_out, rows, (((0,), (1,)), ((), ())), preferred_element_type=jnp.float32
                ).astype(jnp.bfloat16),
                "rep",
                scatter_dimension=0,
                tiled=True,
            )
        )
    cache_hits = slot_target[None, :] == local[:, None]
    cache_keys, cache_values = [
        select_rows(
            cache_hits,
            exchange(select_rows(slot_hits, rows).reshape(shards, chunk, width_dev)).reshape(
                tok_rows, width_dev
            ),
        )
        for rows in (key_flat, value_half)
    ]
    mixed_rows = jnp.concatenate([rows.astype(jnp.float32).T for rows in mixed], axis=0)
    mixed_sums = lax.psum(jnp.sum(mixed_rows * mixed_rows, axis=1), "rep")
    normed_rows = (
        mixed_rows * lax.rsqrt(mixed_sums / full_width + EPSILON)[:, None] * post_gain[None, :]
    )
    output = (packed_hidden.astype(jnp.float32) + normed_rows).astype(jnp.bfloat16)
    return (output, cache_keys, cache_values)


def solution(mesh):
    def pick(*operands):
        heads_dev = operands[0].shape[1] // HEAD_DIM
        fits = heads_dev == mesh.shape["tok"] and mesh.shape["rep"] == 4
        chosen = body_heads if fits else body
        return chosen(*operands)

    return jax.shard_map(
        pick,
        mesh=mesh,
        in_specs=(
            P("tok", "rep"),
            P(None, "rep"),
            P(None, "rep"),
            P(None, "rep"),
            P("rep", None),
            P("rep"),
            P("rep"),
            P("rep"),
            P(),
            P(),
            P(),
            P(),
            P(),
        ),
        out_specs=(P("tok", "rep"), P("tok", "rep"), P("tok", "rep")),
        check_vma=False,
    )
```

```python
import functools
import math

import jax
import jax.numpy as jnp
from jax import lax
from jax.experimental import pallas as pl
from jax.experimental.pallas import tpu as pltpu
from jax.sharding import PartitionSpec as P

HEAD_DIM = 128


EPSILON = 1e-06
ROPE_BASE = 500000.0


def rotate(values, positions):
    half_size = values.shape[-1] // 2
    frequency = ROPE_BASE ** (-jnp.arange(half_size, dtype=jnp.float32) * 2.0 / values.shape[-1])
    angles = positions.astype(jnp.float32)[:, None] * frequency[None, :]
    cosine = jnp.cos(angles)[:, None, :]
    sine_part = jnp.sin(angles)[:, None, :]
    lower_half = values[..., :half_size]
    upper_half = values[..., half_size:]
    return jnp.concatenate(
        [
            lower_half * cosine - upper_half * sine_part,
            upper_half * cosine + lower_half * sine_part,
        ],
        axis=-1,
    )


def bucketed(table_rows, row_order, shards):
    picked = table_rows[row_order]
    return picked.reshape(shards, picked.shape[0] // shards, picked.shape[1])


def placement_order(sources, shard_rows):
    local_ids = jnp.arange(sources.shape[0], dtype=jnp.int32)
    arrival = jnp.argsort(sources * shard_rows + local_ids)
    return jnp.argsort(arrival)


def body(
    hidden_in,
    w_query,
    w_key,
    w_value,
    w_out,
    q_gain,
    k_gain,
    post_gain,
    prompt_lengths,
    segment_ids,
    deal,
    inverse,
    slots,
):
    tok_rows, width_dev = hidden_in.shape
    full_width = w_query.shape[0]
    head_size = HEAD_DIM
    heads_dev = width_dev // head_size
    shards = lax.axis_size("tok")
    first_row = lax.axis_index("tok") * tok_rows
    my_packed = lax.dynamic_slice_in_dim(deal, first_row, tok_rows)
    my_segment = segment_ids[my_packed]
    prompt_ids = jnp.arange(prompt_lengths.shape[0], dtype=jnp.int32)
    prompt_starts = jnp.cumsum(prompt_lengths) - prompt_lengths
    my_start = jnp.sum(
        jnp.where(my_segment[:, None] == prompt_ids[None, :], prompt_starts[None, :], 0), axis=1
    )
    positions = my_packed - my_start
    pieces = lax.all_gather(hidden_in, "rep", axis=1, tiled=True)
    query_rows = jnp.dot(pieces, w_query, preferred_element_type=jnp.float32)
    key_rows = jnp.dot(pieces, w_key, preferred_element_type=jnp.float32)
    value_rows = jnp.dot(pieces, w_value, preferred_element_type=jnp.float32)
    query_sums, key_sums = lax.psum(
        (jnp.sum(query_rows * query_rows, axis=1), jnp.sum(key_rows * key_rows, axis=1)), "rep"
    )
    query_rows = (
        query_rows * lax.rsqrt(query_sums / full_width + EPSILON)[:, None] * q_gain[None, :]
    )
    key_rows = key_rows * lax.rsqrt(key_sums / full_width + EPSILON)[:, None] * k_gain[None, :]
    query_rot = rotate(query_rows.reshape(tok_rows, heads_dev, head_size), positions).astype(
        jnp.bfloat16
    )
    key_rot = (
        rotate(key_rows.reshape(tok_rows, heads_dev, head_size), positions)
        .astype(jnp.bfloat16)
        .reshape(tok_rows, width_dev)
    )
    value_half = value_rows.astype(jnp.bfloat16)
    scale = head_size ** (-0.5)

    def attend(state_now, key_block, value_block, key_packed):
        row_top, totals, weighted = state_now
        block_keys = key_block.reshape(key_block.shape[0], heads_dev, head_size)
        block_values = value_block.reshape(value_block.shape[0], heads_dev, head_size)
        key_segment = segment_ids[key_packed]
        allowed = (key_segment[None, :] == my_segment[:, None]) & (
            key_packed[None, :] <= my_packed[:, None]
        )
        scores = (
            jnp.einsum("qhd,khd->hqk", query_rot, block_keys, preferred_element_type=jnp.float32)
            * scale
        )
        masked = jnp.where(allowed[None], scores, -1e30)
        new_top = jnp.maximum(row_top, jnp.max(masked, axis=2))
        weights = jnp.where(allowed[None], jnp.exp(masked - new_top[:, :, None]), 0.0)
        factor = jnp.exp(row_top - new_top)
        totals = totals * factor + jnp.sum(weights, axis=2)
        weighted = weighted * factor[:, :, None] + jnp.einsum(
            "hqk,khd->hqd",
            weights.astype(jnp.bfloat16),
            block_values,
            preferred_element_type=jnp.float32,
        )
        return (new_top, totals, weighted)

    start_state = (
        jnp.full((heads_dev, tok_rows), -1e30, jnp.float32),
        jnp.zeros((heads_dev, tok_rows), jnp.float32),
        jnp.zeros((heads_dev, tok_rows, head_size), jnp.float32),
    )
    owned_rows = lax.dynamic_slice_in_dim(jnp.argsort(slots), first_row, tok_rows)
    my_slots = lax.dynamic_slice_in_dim(slots, first_row, tok_rows)
    slot_order = jnp.argsort(my_slots)
    sent_keys, sent_values = (
        lax.all_to_all(
            bucketed(key_rot, slot_order, shards), "tok", split_axis=0, concat_axis=0, tiled=True
        ),
        lax.all_to_all(
            bucketed(value_half, slot_order, shards), "tok", split_axis=0, concat_axis=0, tiled=True
        ),
    )
    arrival = placement_order(owned_rows // tok_rows, tok_rows)
    cache_keys = sent_keys.reshape(tok_rows, width_dev)[arrival]
    cache_values = sent_values.reshape(tok_rows, width_dev)[arrival]
    pieces = (
        lax.all_gather(key_rot, "tok", axis=0, tiled=True),
        lax.all_gather(value_half, "tok", axis=0, tiled=True),
    )
    key_all = pieces[0]
    block_size = math.gcd(key_all.shape[0], tok_rows)
    block_count = key_all.shape[0] // block_size

    def advance(state_in, block_set):
        return (attend(state_in, block_set[0], block_set[1], block_set[2]), None)

    state_out, _ = lax.scan(
        advance,
        start_state,
        (
            key_all.reshape(block_count, block_size, width_dev),
            pieces[1].reshape(block_count, block_size, width_dev),
            deal.reshape(block_count, block_size),
        ),
    )
    row_top, totals, weighted = state_out
    attended = (
        (weighted / totals[:, :, None])
        .transpose(1, 0, 2)
        .reshape(tok_rows, width_dev)
        .astype(jnp.bfloat16)
    )
    mixed_rows = (
        lax.psum_scatter(
            lax.dot_general(
                w_out, attended, (((0,), (1,)), ((), ())), preferred_element_type=jnp.float32
            ).astype(jnp.bfloat16),
            "rep",
            scatter_dimension=0,
            tiled=True,
        )
        .astype(jnp.float32)
        .T
    )
    mixed_sums = lax.psum(jnp.sum(mixed_rows * mixed_rows, axis=1), "rep")
    normed_rows = (
        mixed_rows * lax.rsqrt(mixed_sums / full_width + EPSILON)[:, None] * post_gain[None, :]
    )
    result_rows = (hidden_in.astype(jnp.float32) + normed_rows).astype(jnp.bfloat16)
    packed_order = jnp.argsort(my_packed)
    returned = lax.all_to_all(
        bucketed(result_rows, packed_order, shards), "tok", split_axis=0, concat_axis=0, tiled=True
    )
    my_dealt = lax.dynamic_slice_in_dim(inverse, first_row, tok_rows)
    output = returned.reshape(tok_rows, width_dev)[placement_order(my_dealt // tok_rows, tok_rows)]
    return (output, cache_keys, cache_values)


def select_rows(hits, rows):
    return jnp.dot(
        hits.astype(jnp.bfloat16), rows, preferred_element_type=jnp.float32
    ).astype(jnp.bfloat16)


def attend_kernel(
    starts_ref, target_ref, qk_ref, v_ref, out_ref, keys, values, *, size, head_size, part, parts
):
    share = size // parts
    skip = part * share
    block = pl.program_id(0)
    mine = pl.ds(pl.multiple_of(block * size, size), size)
    row_iota = lax.broadcasted_iota(jnp.int32, (size, size), 0)
    hits = jnp.where(row_iota == target_ref[0], 1.0, 0.0).astype(jnp.bfloat16)
    qk_rows = qk_ref[...].reshape(size, 2 * head_size)
    v_rows = v_ref[...].reshape(size, head_size)
    packed_qk = jnp.dot(hits, qk_rows, preferred_element_type=jnp.float32).astype(jnp.bfloat16)
    packed_v = jnp.dot(hits, v_rows, preferred_element_type=jnp.float32).astype(jnp.bfloat16)
    query = packed_qk[skip : skip + share, :head_size]
    keys[mine, :] = packed_qk[:, head_size:]
    values[mine, :] = packed_v
    base_row = block * size
    first = base_row + skip
    rows = first + lax.broadcasted_iota(jnp.int32, (share, 1), 0)
    row_start = jnp.zeros((share, 1), jnp.int32)
    low = jnp.int32(0)
    for prompt in range(starts_ref.shape[0]):
        start = starts_ref[prompt]
        row_start = jnp.where(rows >= start, jnp.maximum(row_start, start), row_start)
        low = jnp.where(first >= start, jnp.maximum(low, start), low)
    scale = head_size ** (-0.5) * math.log2(math.e)

    def scores_of(key_rows):
        return lax.dot_general(
            query, key_rows, (((1,), (1,)), ((), ())), preferred_element_type=jnp.float32
        ) * scale

    column_iota = lax.broadcasted_iota(jnp.int32, (share, size), 1)
    row_iota = lax.broadcasted_iota(jnp.int32, (share, size), 0)
    allowed = (column_iota >= row_start - base_row) & (column_iota <= row_iota + skip)
    scores = jnp.where(allowed, scores_of(packed_qk[:, head_size:]), -1e30)
    top = jnp.max(scores, axis=1, keepdims=True)
    weights = jnp.exp2(scores - top)
    totals = jnp.sum(weights, axis=1, keepdims=True)
    weighted = jnp.dot(
        weights.astype(jnp.bfloat16), packed_v, preferred_element_type=jnp.float32
    )

    def earlier(step, state):
        top, totals, weighted = state
        base = pl.multiple_of((block - 1 - step) * size, size)
        scores = scores_of(keys[pl.ds(base, size), :])
        scores = jnp.where(column_iota >= row_start - base, scores, -1e30)
        new_top = jnp.maximum(top, jnp.max(scores, axis=1, keepdims=True))
        factor = jnp.exp2(top - new_top)
        weights = jnp.exp2(scores - new_top)
        totals = totals * factor + jnp.sum(weights, axis=1, keepdims=True)
        weighted = weighted * factor + jnp.dot(
            weights.astype(jnp.bfloat16),
            values[pl.ds(base, size), :],
            preferred_element_type=jnp.float32,
        )
        return (new_top, totals, weighted)

    top, totals, weighted = lax.fori_loop(
        0, block - low // size, earlier, (top, totals, weighted)
    )
    out_ref[...] = (weighted / totals).astype(jnp.bfloat16)


def attend_head(starts, target, qk_rows, v_rows, part, parts):
    shards, tok_rows, head_size = v_rows.shape
    chunk = tok_rows // shards
    return pl.pallas_call(
        functools.partial(
            attend_kernel, size=tok_rows, head_size=head_size, part=part, parts=parts
        ),
        out_shape=jax.ShapeDtypeStruct((shards * tok_rows // parts, head_size), jnp.bfloat16),
        grid_spec=pltpu.PrefetchScalarGridSpec(
            num_scalar_prefetch=1,
            grid=(shards,),
            in_specs=[
                pl.BlockSpec((1, 1, tok_rows), lambda i, s: (i, 0, 0)),
                pl.BlockSpec((shards, chunk, 2 * head_size), lambda i, s: (0, i, 0)),
                pl.BlockSpec((shards, chunk, head_size), lambda i, s: (0, i, 0)),
            ],
            out_specs=pl.BlockSpec((tok_rows // parts, head_size), lambda i, s: (i, 0)),
            scratch_shapes=[
                pltpu.VMEM((shards * tok_rows, head_size), jnp.bfloat16),
                pltpu.VMEM((shards * tok_rows, head_size), jnp.bfloat16),
            ],
        ),
        compiler_params=pltpu.CompilerParams(
            dimension_semantics=("arbitrary",), vmem_limit_bytes=48 << 20
        ),
        cost_estimate=pl.CostEstimate(
            flops=8 * tok_rows * tok_rows * shards * head_size * 3 // parts,
            bytes_accessed=8 * shards * tok_rows * head_size,
            transcendentals=3 * shards * tok_rows * tok_rows,
        ),
    )(starts, target, qk_rows, v_rows)


def rope_kernel(q_ref, k_ref, q_scale, k_scale, q_gain, k_gain, cosine, sine, qk_ref, key_ref):
    head_size = q_ref.shape[1]

    def turned(rows, scale, gain):
        normed = rows[...] * scale[...] * gain[...]
        other = pltpu.roll(normed, head_size // 2, 1)
        return (normed * cosine[...] + other * sine[...]).astype(jnp.bfloat16)

    qk_ref[0, :, :head_size] = turned(q_ref, q_scale, q_gain)
    key_rows = turned(k_ref, k_scale, k_gain)
    qk_ref[0, :, head_size:] = key_rows
    key_ref[...] = key_rows


def rope_heads(query_rows, key_rows, q_scale, k_scale, q_gain, k_gain, cosine, sine):
    rows, width = query_rows.shape
    head_size = cosine.shape[1]
    heads = width // head_size
    wide = pl.BlockSpec((rows, head_size), lambda h: (0, h))
    thin = pl.BlockSpec((rows, 1), lambda h: (0, 0))
    gain = pl.BlockSpec((1, head_size), lambda h: (0, h))
    table = pl.BlockSpec((rows, head_size), lambda h: (0, 0))
    return pl.pallas_call(
        rope_kernel,
        out_shape=(
            jax.ShapeDtypeStruct((heads, rows, 2 * head_size), jnp.bfloat16),
            jax.ShapeDtypeStruct((rows, width), jnp.bfloat16),
        ),
        grid=(heads,),
        in_specs=[wide, wide, thin, thin, gain, gain, table, table],
        out_specs=(pl.BlockSpec((1, rows, 2 * head_size), lambda h: (h, 0, 0)), wide),
        compiler_params=pltpu.CompilerParams(vmem_limit_bytes=24 << 20),
        cost_estimate=pl.CostEstimate(
            flops=14 * rows * width, bytes_accessed=14 * rows * width, transcendentals=0
        ),
    )(query_rows, key_rows, q_scale, k_scale, q_gain, k_gain, cosine, sine)


def value_kernel(owner_ref, x_ref, w_ref, so_far_ref, flat_ref, heads_ref):
    rows = so_far_ref[...] + jnp.dot(x_ref[...], w_ref[...], preferred_element_type=jnp.float32)
    rows = rows.astype(jnp.bfloat16)
    flat_ref[...] = rows
    count, _, head_size = heads_ref.shape
    for head in range(count):
        heads_ref[head] = rows[:, head * head_size : (head + 1) * head_size]


def value_heads(owner, pieces, w_value, so_far, head_size):
    rows, depth = pieces.shape
    width = w_value.shape[1]
    count = 2
    return pl.pallas_call(
        value_kernel,
        out_shape=(
            jax.ShapeDtypeStruct((rows, width), jnp.bfloat16),
            jax.ShapeDtypeStruct((width // head_size, rows, head_size), jnp.bfloat16),
        ),
        grid_spec=pltpu.PrefetchScalarGridSpec(
            num_scalar_prefetch=1,
            grid=(width // (count * head_size),),
            in_specs=[
                pl.BlockSpec((rows, depth), lambda h, owner: (0, 0)),
                pl.BlockSpec((depth, count * head_size), lambda h, owner: (owner[0], h)),
                pl.BlockSpec((rows, count * head_size), lambda h, owner: (0, h)),
            ],
            out_specs=(
                pl.BlockSpec((rows, count * head_size), lambda h, owner: (0, h)),
                pl.BlockSpec((count, rows, head_size), lambda h, owner: (h, 0, 0)),
            ),
        ),
        compiler_params=pltpu.CompilerParams(vmem_limit_bytes=40 << 20),
        cost_estimate=pl.CostEstimate(
            flops=2 * rows * depth * width,
            bytes_accessed=2 * (rows * depth + depth * width + 2 * rows * width),
            transcendentals=0,
        ),
    )(owner, pieces, w_value, so_far)


def body_heads(
    hidden_in,
    w_query,
    w_key,
    w_value,
    w_out,
    q_gain,
    k_gain,
    post_gain,
    prompt_lengths,
    segment_ids,
    deal,
    inverse,
    slots,
):
    tok_rows, width_dev = hidden_in.shape
    full_width = w_query.shape[0]
    head_size = HEAD_DIM
    heads_dev = width_dev // head_size
    shards = lax.axis_size("tok")
    chunk = tok_rows // shards
    me = lax.axis_index("tok")
    first_row = me * tok_rows
    half_rows = tok_rows // 2
    corner = lax.axis_index("rep")
    across = [(i, i ^ 1) for i in range(4)]
    along = [(i, i ^ 2) for i in range(4)]

    local = jnp.arange(tok_rows, dtype=jnp.int32)
    starts = jnp.cumsum(prompt_lengths) - prompt_lengths
    my_packed = lax.dynamic_slice_in_dim(deal, first_row, tok_rows)
    my_slots = lax.dynamic_slice_in_dim(slots, first_row, tok_rows)
    rank = jnp.sum((my_packed[None, :] < my_packed[:, None]).astype(jnp.int32), axis=1)
    sort_hits = rank[None, :] == local[:, None]
    sorted_packed = jnp.sum(jnp.where(sort_hits, my_packed[None, :], 0), axis=1)
    sorted_slots = jnp.sum(jnp.where(sort_hits, my_slots[None, :], 0), axis=1)
    my_start = jnp.max(
        jnp.where(starts[None, :] <= sorted_packed[:, None], starts[None, :], 0), axis=1
    )
    positions = sorted_packed - my_start

    source = inverse.reshape(shards, tok_rows) // tok_rows
    before = (source[:, None, :] == source[:, :, None]) & (local[None, None, :] < local[None, :, None])
    arrived = source * chunk + jnp.sum(before.astype(jnp.int32), axis=2)
    target = jnp.sum(
        jnp.where(arrived[:, :, None] == local[None, None, :], local[None, :, None], 0), axis=1
    )

    slot_rank = jnp.sum((sorted_slots[None, :] < sorted_slots[:, None]).astype(jnp.int32), axis=1)
    slot_hits = slot_rank[None, :] == local[:, None]
    slot_rows = slots.reshape(shards, tok_rows) - first_row
    owned = (slot_rows >= 0) & (slot_rows < tok_rows)
    ahead = owned[:, None, :] & (slot_rows[:, None, :] < slot_rows[:, :, None])
    landed = jnp.arange(shards, dtype=jnp.int32)[:, None] * chunk + jnp.sum(
        ahead.astype(jnp.int32), axis=2
    )
    landed = jnp.where(owned, landed, -1).reshape(-1)
    slot_target = jnp.sum(
        jnp.where(landed[:, None] == local[None, :], slot_rows.reshape(-1)[:, None], 0), axis=0
    )

    piece = select_rows(sort_hits, hidden_in)
    piece_x = lax.ppermute(piece, "rep", across)
    piece_y = lax.ppermute(piece, "rep", along)
    piece_xy = jnp.concatenate(
        [
            lax.ppermute(piece_y[:half_rows], "rep", across),
            lax.ppermute(piece_x[half_rows:], "rep", along),
        ],
        axis=0,
    )

    def product(rows, weights, step):
        owned = lax.dynamic_slice_in_dim(weights, (corner ^ step) * width_dev, width_dev, axis=0)
        return jnp.dot(rows, owned, preferred_element_type=jnp.float32)

    sums_now = [product(piece, weights, 0) for weights in (w_value, w_query, w_key)]
    for step, rows in ((1, piece_x), (2, piece_y)):
        sums_now = [
            done + product(rows, weights, step)
            for done, weights in zip(sums_now, (w_value, w_query, w_key))
        ]

    sent_hidden = lax.all_to_all(
        piece.reshape(shards, chunk, width_dev),
        "tok",
        split_axis=0,
        concat_axis=0,
        tiled=True,
    )
    half_size = head_size // 2
    frequency = ROPE_BASE ** (-jnp.arange(half_size, dtype=jnp.float32) * 2.0 / head_size)
    angles = positions.astype(jnp.float32)[:, None] * frequency[None, :]
    cosine, sine = jnp.cos(angles), jnp.sin(angles)
    cosine = jnp.concatenate([cosine, cosine], axis=1)
    sine = jnp.concatenate([-sine, sine], axis=1)
    piece_xy, sent_hidden, cosine, sine, target, slot_target, sums_now = lax.optimization_barrier(
        (piece_xy, sent_hidden, cosine, sine, target, slot_target, sums_now)
    )
    my_target = lax.dynamic_index_in_dim(target, me, 0, keepdims=False)
    my_hits = my_target[None, :] == local[:, None]

    last = corner ^ 3
    value_half, value_sent = value_heads(last[None], piece_xy, w_value, sums_now[0], head_size)

    def exchange(rows):
        return lax.all_to_all(rows, "tok", split_axis=0, concat_axis=0, tiled=True)

    v_rows = exchange(value_sent)
    piece_xy, value_half = lax.optimization_barrier((piece_xy, value_half))
    query_rows = sums_now[1] + product(piece_xy, w_query, 3)
    key_rows = sums_now[2] + product(piece_xy, w_key, 3)
    sums = jnp.stack(
        [jnp.sum(query_rows * query_rows, axis=1), jnp.sum(key_rows * key_rows, axis=1)]
    )
    scales = lax.rsqrt(lax.psum(sums, "rep") / full_width + EPSILON)
    qk_sent, key_flat = rope_heads(
        query_rows,
        key_rows,
        scales[0][:, None],
        scales[1][:, None],
        q_gain[None, :],
        k_gain[None, :],
        cosine,
        sine,
    )
    qk_rows = exchange(qk_sent)
    qk_rows, v_rows, sent_hidden = lax.optimization_barrier((qk_rows, v_rows, sent_hidden))
    packed_hidden = select_rows(my_hits, sent_hidden.reshape(tok_rows, width_dev))

    parts = 2
    share = tok_rows // parts
    heads_out = [
        attend_head(starts, target[:, None, :], qk_rows, v_rows, part, parts).reshape(
            shards, share, head_size
        )
        for part in range(parts)
    ]
    first, last = lax.optimization_barrier((exchange(heads_out[0]), heads_out[1]))
    attended = [first, exchange(last)]
    attended[-1], key_flat, value_half = lax.optimization_barrier(
        (attended[-1], key_flat, value_half)
    )
    mixed = []
    for rows in attended:
        rows = rows.transpose(1, 0, 2).reshape(share, width_dev)
        mixed.append(
            lax.psum_scatter(
                lax.dot_general(
                    w_out, rows, (((0,), (1,)), ((), ())), preferred_element_type=jnp.float32
                ).astype(jnp.bfloat16),
                "rep",
                scatter_dimension=0,
                tiled=True,
            )
        )
    cache_hits = slot_target[None, :] == local[:, None]
    sent_keys, sent_values = [
        exchange(select_rows(slot_hits, rows).reshape(shards, chunk, width_dev)).reshape(
            tok_rows, width_dev
        )
        for rows in (key_flat, value_half)
    ]
    mixed_rows = jnp.concatenate([rows.astype(jnp.float32).T for rows in mixed], axis=0)
    mixed_sums = lax.psum(jnp.sum(mixed_rows * mixed_rows, axis=1), "rep")
    normed_rows = (
        mixed_rows * lax.rsqrt(mixed_sums / full_width + EPSILON)[:, None] * post_gain[None, :]
    )
    output = (packed_hidden.astype(jnp.float32) + normed_rows).astype(jnp.bfloat16)
    output, sent_keys = lax.optimization_barrier((output, sent_keys))
    cache_keys = select_rows(cache_hits, sent_keys)
    cache_values = select_rows(cache_hits, sent_values)
    return (output, cache_keys, cache_values)


def solution(mesh):
    def pick(*operands):
        heads_dev = operands[0].shape[1] // HEAD_DIM
        fits = heads_dev == mesh.shape["tok"] and mesh.shape["rep"] == 4
        chosen = body_heads if fits else body
        return chosen(*operands)

    return jax.shard_map(
        pick,
        mesh=mesh,
        in_specs=(
            P("tok", "rep"),
            P(None, "rep"),
            P(None, "rep"),
            P(None, "rep"),
            P("rep", None),
            P("rep"),
            P("rep"),
            P("rep"),
            P(),
            P(),
            P(),
            P(),
            P(),
        ),
        out_specs=(P("tok", "rep"), P("tok", "rep"), P("tok", "rep")),
        check_vma=False,
    )
```
